32 devices in a mesh: grp: 2 (over y), row: 4 (over z), col: 2 (over x), rep: 2 (over core).
Axes of the slice: x: 2, y: 2, z: 4, core: 2. Of those that a mesh axis runs over, the one named last changes fastest.
Arguments:
- emb_row: bfloat16 [2048, 1280], P(('grp', 'row', 'rep'), 'col'), parts along dimension 0, may hold values from -6 to 6
- emb_col: bfloat16 [512, 1280], P(('grp', 'col'), 'row'), parts along dimension 0, may hold values from -6 to 6
- proj_row: bfloat16 [1280, 64], replicated, may hold values from -0.15625 to 0.15625
- proj_col: bfloat16 [1280, 64], replicated, may hold values from -0.15625 to 0.15625
- pair_out: bfloat16 [64, 64], replicated, may hold values from -0.75 to 0.75
- pair_bias: float32 [64], replicated, may hold values from -3 to 3
- conv_weight: bfloat16 [3, 3, 64, 64], replicated, may hold values from -0.25 to 0.25
- conv_bias: float32 [64], replicated, may hold values from -3 to 3
- target: bfloat16 [64, 2048, 256], P(None, ('grp', 'row', 'rep'), 'col'), parts along dimension 1, may hold values from -6 to 6
- kept_tiles: int32 [16, 2], P(('grp', 'row', 'rep'), 'col'), parts along dimension 0, may hold values 0 or 1
Outputs:
- cell_loss: float32 [2048, 256], P(('grp', 'row', 'rep'), 'col'), parts along dimension 0
- grad_conv: float32 [6, 3, 64, 64], P('grp'), parts along dimension 0
- grad_bias: float32 [128], P('grp'), parts along dimension 0
The draws below stay inside these ranges and needn't reach their ends.
There are 2 independent parts, one for each index of `grp`. The reference program is written for one: setup_inputs(seed, part) draws one part's arguments, and reference() takes and returns one part's arrays. A program takes and returns all parts, laid end to end along the dimension named above; an argument that names none is the same for every part. Nothing has to cross between parts.
All inputs are finite; a program needn't handle non-finite values. No bound on the sum of `kept_tiles` on one device may be relied on, other than what follows from the above.
Results may differ from the reference program's by a relative error of at most 0.0025.
Values may be sent and summed in bfloat16 or wider, within the bound.
A program may use at most 128 MiB of HBM per device.

```python
import jax
import jax.numpy as jnp
from jax import lax

EMBED = 1280
RANK = 64
CHANNELS = 64
TILE_EDGE = 128
ROWS_ALL = 1024
COLS_ALL = 256
TILE_ROWS = 8
TILE_COLS = 2


def touch_ends(result, rng, least, high):
    index_at = [jax.random.randint(jax.random.fold_in(rng, axis), (), 0, length) for axis, length in enumerate(result.shape)]
    widest = result.shape.index(max(result.shape))
    next_to = index_at[:widest] + [(index_at[widest] + 1) % result.shape[widest]] + index_at[widest + 1:]
    return result.at[tuple(index_at)].set(least).at[tuple(next_to)].set(high)


def block_scale(own_key, shape, pieces, least, largest):
    def one(dim, shards_of):
        draws = jax.random.uniform(jax.random.fold_in(jax.random.fold_in(own_key, 6), dim), (shards_of,), jnp.float32, least / len(pieces), largest / len(pieces))
        return jnp.repeat(jnp.exp(draws), shape[dim] // shards_of).reshape((-1,) + (1,) * (len(shape) - dim - 1))

    gain = one(*pieces[0])
    for cut in pieces[1:]:
        gain = gain * one(*cut)
    return gain


def centred(key, extent, scale, bound, cuts=(), held_as=jnp.bfloat16):
    values = jax.random.normal(key, extent, jnp.float32) * scale
    if len(cuts) > 0:
        values = block_scale(key, extent, cuts, -0.22, 0.18) * values
    return jnp.clip(values, min=-bound, max=bound).astype(held_as)


def setup_inputs(seed: int = 0, part: int = 0) -> dict:
    key_list = jax.random.split(jax.random.key(seed), 11)
    own_keys = jax.random.split(jax.random.fold_in(key_list[10], part), 11)
    return {
        "emb_row": centred(own_keys[0], (ROWS_ALL, EMBED), 1.0, 6.0, ((0, 8), (1, 2))),
        "emb_col": centred(own_keys[1], (COLS_ALL, EMBED), 1.0, 6.0, ((0, 2), (1, 4))),
        "proj_row": centred(key_list[2], (EMBED, RANK), EMBED ** -0.5, 0.15625),
        "proj_col": centred(key_list[3], (EMBED, RANK), EMBED ** -0.5, 0.15625),
        "pair_out": centred(key_list[4], (RANK, CHANNELS), RANK ** -0.5, 0.75),
        "pair_bias": centred(key_list[5], (CHANNELS,), 0.5, 3.0, (), jnp.float32),
        "conv_weight": centred(key_list[6], (3, 3, CHANNELS, CHANNELS), (9 * CHANNELS) ** -0.5, 0.25),
        "conv_bias": centred(key_list[7], (CHANNELS,), 0.5, 3.0, (), jnp.float32),
        "target": centred(own_keys[8], (CHANNELS, ROWS_ALL, COLS_ALL), 1.0, 6.0, ((1, 8), (2, 2))),
        "kept_tiles": touch_ends((jax.random.randint(own_keys[9], (TILE_ROWS, TILE_COLS), 0, 4) < 3).astype(jnp.int32), jax.random.fold_in(own_keys[9], 1), 0, 1),
    }


def expand_tiles(tiles, edge):
    count_r, count_c = tiles.shape
    wide = jnp.broadcast_to(tiles.astype(jnp.float32)[:, None, :, None], (count_r, edge, count_c, edge))
    return wide.reshape(count_r * edge, count_c * edge)


def block_terms(padded, pair_feat, target_part, mask, conv_weight, conv_bias):
    rows = pair_feat.shape[1]
    width = pair_feat.shape[2]
    conv_out = jnp.broadcast_to(conv_bias[:, None, None], pair_feat.shape)
    for row_tap in range(3):
        for col_tap in range(3):
            window = padded[:, 2 * row_tap:2 * row_tap + rows, 2 * col_tap:2 * col_tap + width].astype(jnp.float32)
            conv_out = conv_out + jnp.einsum("co,cij->oij", conv_weight[row_tap, col_tap].astype(jnp.float32), window)
    differ = mask[None] * (pair_feat + conv_out - target_part.astype(jnp.float32))
    loss_part = 0.5 * jnp.sum(differ * differ, axis=0)
    grad_in = differ.astype(jnp.bfloat16).astype(jnp.float32)
    taps = []
    for row_tap in range(3):
        for col_tap in range(3):
            window = padded[:, 2 * row_tap:2 * row_tap + rows, 2 * col_tap:2 * col_tap + width].astype(jnp.float32)
            taps.append(jnp.einsum("cij,oij->co", window, grad_in))
    grads = jnp.stack(taps).reshape(3, 3, pair_feat.shape[0], pair_feat.shape[0])
    return loss_part, grads, jnp.sum(differ, axis=(1, 2))


def reference(emb_row, emb_col, proj_row, proj_col, pair_out, pair_bias, conv_weight, conv_bias, target, kept_tiles):
    row_feat = jnp.dot(emb_row, proj_row, preferred_element_type=jnp.float32).astype(jnp.bfloat16)
    col_feat = jnp.dot(emb_col, proj_col, preferred_element_type=jnp.float32).astype(jnp.bfloat16)
    mask = expand_tiles(kept_tiles, TILE_EDGE)
    row_pad = jnp.pad(row_feat, ((2, 2), (0, 0)))
    mask_pad = jnp.pad(mask, ((2, 2), (0, 0)))
    col_wide = col_feat.astype(jnp.float32)
    out_wide = pair_out.astype(jnp.float32)

    def one_block(index):
        start = (index * TILE_EDGE).astype(jnp.int32)
        feats = lax.dynamic_slice_in_dim(row_pad, start, TILE_EDGE + 4, 0)
        mask_rows = lax.dynamic_slice_in_dim(mask_pad, start, TILE_EDGE + 4, 0)
        scaled = (out_wide.T[:, :, None] * feats.astype(jnp.float32).T[None, :, :]).astype(jnp.bfloat16)
        feat_ext = jnp.einsum("cki,jk->cij", scaled.astype(jnp.float32), col_wide) + pair_bias[:, None, None]
        hidden = (jnp.maximum(feat_ext, 0.0) * mask_rows[None]).astype(jnp.bfloat16)
        padded = jnp.pad(hidden, ((0, 0), (0, 0), (2, 2)))
        pair_feat = feat_ext[:, 2:TILE_EDGE + 2]
        mask_here = mask_rows[2:TILE_EDGE + 2]
        target_part = lax.dynamic_slice_in_dim(target, start, TILE_EDGE, 1)
        return block_terms(padded, pair_feat, target_part, mask_here, conv_weight, conv_bias)

    losses, grads, biases = lax.map(one_block, jnp.arange(ROWS_ALL // TILE_EDGE).astype(jnp.int32))
    norm = 1.0 / (TILE_EDGE * TILE_EDGE)
    cell_loss = losses.reshape(ROWS_ALL, COLS_ALL)
    return cell_loss, jnp.sum(grads, axis=0) * norm, jnp.sum(biases, axis=0) * norm
```

```python
import functools

import jax
import jax.numpy as jnp
from jax import lax
from jax.experimental import pallas as pl
from jax.experimental.pallas import tpu as pltpu
from jax.sharding import PartitionSpec as P

MESH = pl.DeviceIdType.MESH
F32 = jnp.float32
BF16 = jnp.bfloat16
NT = (((1,), (1,)), ((), ()))


def loop(low, high, body):
    if high - low <= 16:
        for d in range(low, high):
            body(d)
    else:
        lax.fori_loop(low, high, lambda d, _: (body(d), 0)[1], 0)


def kernel(
    sizes,
    emb_row,
    emb_col,
    proj_row,
    proj_col,
    pair_out,
    pair_bias,
    conv_weight,
    conv_bias,
    target,
    kept,
    loss_out,
    conv_grad_out,
    bias_out,
    rowbuf,
    rowedge,
    colbuf,
    coledge,
    row_feat,
    col_wide,
    wide_t,
    target32,
    hid,
    base,
    grad_in,
    weight_f,
    total,
    bias_acc,
    part,
    reduced,
    full,
    row_send,
    row_recv,
    redge_send,
    redge_recv,
    col_send,
    col_recv,
    cedge_send,
    cedge_recv,
    rs_send,
    rs_recv,
    ag_send,
    ag_recv,
):
    n_row, n_col, n_rep, edge, chan, chunk = sizes
    n_all = n_row * n_col * n_rep
    pairs = edge // 2
    row, col, rep = lax.axis_index("row"), lax.axis_index("col"), lax.axis_index("rep")
    line = row * n_rep + rep
    n_line = n_row * n_rep
    me = line * n_col + col

    def device(index):
        across = index % n_col
        along = index // n_col
        return {"row": along // n_rep, "rep": along % n_rep, "col": across}

    barrier = pltpu.get_barrier_semaphore()
    loop(
        1,
        n_all,
        lambda d: pl.semaphore_signal(
            barrier, inc=1, device_id=device((me + d) % n_all), device_id_type=MESH
        ),
    )

    def share(ref, emb, index):
        width = emb.shape[1]
        if ref.shape[0] == width:
            return ref[...]
        return ref[pl.ds(pl.multiple_of(index * width, 16), width), :]

    keep = kept[0, 0].astype(F32)
    part_row = jnp.dot(
        emb_row[...], share(proj_row, emb_row, col), preferred_element_type=F32
    )
    part_col = jnp.dot(
        emb_col[...], share(proj_col, emb_col, row), preferred_element_type=F32
    )
    rank = part_row.shape[1]
    rowbuf[col, 8 : edge + 8, :] = part_row
    rowbuf[col, 0:8, :] = jnp.full((8, rank), keep, F32)
    rowbuf[col, edge + 8 : edge + 16, :] = jnp.full((8, rank), keep, F32)
    colbuf[row, :, :] = part_col

    pl.semaphore_wait(barrier, n_all - 1)

    def row_copy(d, src):
        return pltpu.make_async_remote_copy(
            src_ref=rowbuf.at[src],
            dst_ref=rowbuf.at[src],
            send_sem=row_send.at[d],
            recv_sem=row_recv.at[src],
            device_id={"col": (col + d) % n_col},
            device_id_type=MESH,
        )

    def redge_copy(side, d, src):
        to = (line + (1 if side == 0 else n_line - 1)) % n_line
        return pltpu.make_async_remote_copy(
            src_ref=rowbuf.at[src, pl.ds(edge if side == 0 else 0, 16)],
            dst_ref=rowedge.at[side, src],
            send_sem=redge_send.at[side, d],
            recv_sem=redge_recv.at[side, src],
            device_id={"row": to // n_rep, "rep": to % n_rep, "col": (col + d) % n_col},
            device_id_type=MESH,
        )

    def col_copy(d, src):
        return pltpu.make_async_remote_copy(
            src_ref=colbuf.at[src],
            dst_ref=colbuf.at[src],
            send_sem=col_send.at[d],
            recv_sem=col_recv.at[src],
            device_id={"row": (row + d) % n_row},
            device_id_type=MESH,
        )

    def cedge_copy(side, d, src):
        to = (col + (1 if side == 0 else n_col - 1)) % n_col
        return pltpu.make_async_remote_copy(
            src_ref=colbuf.at[src, pl.ds(edge - 8 if side == 0 else 0, 8)],
            dst_ref=coledge.at[side, src],
            send_sem=cedge_send.at[side, d],
            recv_sem=cedge_recv.at[side, src],
            device_id={"row": (row + d) % n_row, "col": to},
            device_id_type=MESH,
        )

    loop(1, n_row, lambda d: col_copy(d, row).start())
    loop(1, n_col, lambda d: row_copy(d, col).start())
    for side in range(2):
        loop(0, n_row, lambda d: cedge_copy(side, d, row).start())
        loop(0, n_col, lambda d: redge_copy(side, d, col).start())

    def widen(c, _):
        start = pl.multiple_of(c * edge, edge)
        target32[pl.ds(start, edge), :] = target[c].astype(F32)
        return 0

    lax.fori_loop(0, chan, widen, 0, unroll=4)
    for a in range(3):
        for b in range(3):
            weight_f[b * chan : (b + 1) * chan, a * chan : (a + 1) * chan] = conv_weight[
                a, b
            ].astype(F32)
    weight_t = weight_f[...].T.astype(BF16)
    out_t = pair_out[...].astype(F32).T
    pair_b = jnp.broadcast_to(pair_bias[...], (128, chan)).T
    conv_b = jnp.broadcast_to(conv_bias[...], (128, chan)).T
    zeros = jnp.zeros((2 * chan, 2 * edge), BF16)
    grad_in[0 : 2 * chan, :] = zeros
    grad_in[(pairs + 2) * chan : (pairs + 4) * chan, :] = zeros
    base[0 : 2 * chan, :] = zeros.astype(F32)
    base[(pairs + 2) * chan : (pairs + 4) * chan, :] = zeros.astype(F32)
    bias_acc[...] = jnp.zeros_like(bias_acc)
    total[...] = jnp.zeros_like(total)

    loop(1, n_row, lambda d: col_copy(d, (row + n_row - d) % n_row).wait_recv())
    loop(1, n_col, lambda d: row_copy(d, (col + n_col - d) % n_col).wait_recv())
    for side in range(2):
        loop(0, n_row, lambda d: cedge_copy(side, d, (row + n_row - d) % n_row).wait_recv())
        loop(0, n_col, lambda d: redge_copy(side, d, (col + n_col - d) % n_col).wait_recv())

    def rounded(x):
        return x.astype(BF16).astype(F32)

    row_feat[0:8, :] = rounded(sum(rowedge[0, c, 0:8, :] for c in range(n_col)))
    row_feat[8 : edge + 8, :] = rounded(sum(rowbuf[c, 8 : edge + 8, :] for c in range(n_col)))
    row_feat[edge + 8 : edge + 16, :] = rounded(
        sum(rowedge[1, c, 8:16, :] for c in range(n_col))
    )
    col_wide[0:8, :] = sum(coledge[0, r] for r in range(n_row))
    col_wide[8 : edge + 8, :] = sum(colbuf[r] for r in range(n_row))
    col_wide[edge + 8 : edge + 16, :] = sum(coledge[1, r] for r in range(n_row))
    for b in range(3):
        wide_t[b * edge : (b + 1) * edge, :] = col_wide[
            6 + 2 * b : 6 + 2 * b + edge, :
        ].astype(BF16)

    lane = lax.broadcasted_iota(jnp.int32, (1, edge), 1)
    before, after = (col + n_col - 1) % n_col, (col + 1) % n_col
    has_before = (col > 0).astype(F32)
    has_after = (col < n_col - 1).astype(F32)

    def masks(get, valid):
        here, left, right = (
            jnp.broadcast_to(get(c), (1, edge)) * scale
            for c, scale in ((col, valid), (before, valid * has_before), (after, valid * has_after))
        )
        return (jnp.where(lane < 2, left, here), here, jnp.where(lane >= edge - 2, right, here))

    top = masks(lambda c: rowedge[0, c, 8:9, 0:1], (line > 0).astype(F32))
    middle = masks(lambda c: rowbuf[c, 0:1, 0:1], jnp.float32(1))
    bottom = masks(lambda c: rowedge[1, c, 0:1, 0:1], (line < n_line - 1).astype(F32))

    def features(pair, count, mask, inner):
        scaled = []
        for r in range(2 * count):
            feat = row_feat[pl.ds(2 * pair + 8 + r, 1), :]
            scaled.append((out_t * feat).astype(BF16))
        product = lax.dot_general(
            jnp.concatenate(scaled, axis=0), wide_t[...], NT, preferred_element_type=F32
        )
        for r in range(2 * count):
            p = pair + r // 2
            lanes = slice((r % 2) * edge, (r % 2 + 1) * edge)
            for b in range(3):
                value = product[r * chan : (r + 1) * chan, b * edge : (b + 1) * edge] + pair_b
                start = pl.multiple_of((p + 1) * 3 * chan + b * chan, chan)
                hid[pl.ds(start, chan), lanes] = (jnp.maximum(value, 0.0) * mask[b]).astype(BF16)
                if inner and b == 1:
                    aim = target32[pl.ds(2 * pair + r, chan, stride=edge), :]
                    start = pl.multiple_of((p + 2) * chan, chan)
                    base[pl.ds(start, chan), lanes] = (value + conv_b) - aim

    features(-1, 1, top, False)
    features(pairs, 1, bottom, False)
    group = 4

    def feature_step(g, _):
        features(g * group, group, middle, True)
        return 0

    lax.fori_loop(0, pairs // group, feature_step, 0)

    def conv_of(p):
        start = pl.multiple_of((p + 1) * 3 * chan, 3 * chan)
        return jnp.dot(weight_t, hid[pl.ds(start, 3 * chan), :], preferred_element_type=F32)

    def slot(p):
        return pl.ds(pl.multiple_of((p + 2) * chan, chan), chan)

    def spread(p, done):
        y = conv_of(p)
        base[slot(p + 1), :] += y[0:chan]
        base[slot(p), :] += y[chan : 2 * chan]
        if done:
            differ = (base[slot(p - 1), :] + y[2 * chan :]) * keep
            grad_in[slot(p - 1), :] = differ.astype(BF16)
            bias_acc[...] += differ
            loss = 0.5 * jnp.sum(differ * differ, axis=0, keepdims=True)
            loss_out[pl.ds(2 * (p - 1), 1), :] = loss[:, 0:edge]
            loss_out[pl.ds(2 * (p - 1) + 1, 1), :] = loss[:, edge : 2 * edge]

    spread(-1, False)
    spread(0, False)

    def conv_step(g, _):
        for r in range(4):
            spread(1 + g * 4 + r, True)
        return 0

    lax.fori_loop(0, pairs // 4, conv_step, 0)

    def grad_step(g, _):
        value = total[...]
        for r in range(6):
            p = g * 6 + r - 1
            start = pl.multiple_of((p + 1) * 3 * chan, 3 * chan)
            near = pl.multiple_of((p + 1) * chan, chan)
            value = value + lax.dot_general(
                hid[pl.ds(start, 3 * chan), :],
                grad_in[pl.ds(near, 3 * chan), :],
                NT,
                preferred_element_type=F32,
            )
        total[...] = value
        return 0

    lax.fori_loop(0, (pairs + 2) // 6, grad_step, 0)

    norm = 1.0 / (edge * edge)
    half = 3 * chan // 2
    rows = 3 * chan + half
    sums = total[...] * norm
    flat = jnp.concatenate(
        [
            sums[:, 0 : 2 * chan],
            jnp.concatenate([sums[0:half, 2 * chan :], sums[half:, 2 * chan :]], axis=1),
        ],
        axis=0,
    )
    bias_sum = lax.dot_general(
        jnp.ones((8, 2 * edge), F32),
        bias_acc[...] * norm,
        NT,
        precision=lax.Precision.HIGHEST,
        preferred_element_type=F32,
    )
    part[0:rows, :] = flat
    part[rows : rows + 8, :] = jnp.concatenate([bias_sum, bias_sum], axis=1)
    rest = n_all * chunk - rows - 8
    if rest > 0:
        part[rows + 8 :, :] = jnp.zeros((rest, 128), F32)

    def piece(index):
        return pl.ds(pl.multiple_of(index * chunk, 8), chunk)

    def rs_copy(d, to, src):
        return pltpu.make_async_remote_copy(
            src_ref=part.at[piece(to)],
            dst_ref=reduced.at[src],
            send_sem=rs_send.at[d],
            recv_sem=rs_recv.at[src],
            device_id=device(to),
            device_id_type=MESH,
        )

    def ag_copy(d, to, src):
        return pltpu.make_async_remote_copy(
            src_ref=full.at[piece(src)],
            dst_ref=full.at[piece(src)],
            send_sem=ag_send.at[d],
            recv_sem=ag_recv.at[src],
            device_id=device(to),
            device_id_type=MESH,
        )

    loop(1, n_all, lambda d: rs_copy(d, (me + d) % n_all, me).start())
    reduced[me] = part[piece(me), :]
    loop(1, n_all, lambda d: rs_copy(d, (me + d) % n_all, (me + n_all - d) % n_all).wait_recv())
    if n_all <= 16:
        own = sum(reduced[r] for r in range(n_all))
    else:
        own = lax.fori_loop(
            0, n_all, lambda r, x: x + reduced[r], jnp.zeros((chunk, 128), F32)
        )
    full[piece(me), :] = own
    loop(1, n_all, lambda d: ag_copy(d, (me + d) % n_all, me).start())
    loop(1, n_all, lambda d: ag_copy(d, (me + d) % n_all, (me + n_all - d) % n_all).wait_recv())

    for b in range(3):
        low = b * chan
        conv_grad_out[2, b] = full[low : low + chan, 0:chan]
        conv_grad_out[1, b] = full[low : low + chan, chan : 2 * chan]
    low = 3 * chan
    conv_grad_out[0, 0] = full[low : low + chan, 0:chan]
    conv_grad_out[0, 1, 0 : half - chan] = full[low + chan : low + half, 0:chan]
    conv_grad_out[0, 1, half - chan :] = full[low : low + 2 * chan - half, chan : 2 * chan]
    conv_grad_out[0, 2] = full[low + 2 * chan - half : low + half, chan : 2 * chan]
    bias_out[...] = full[rows : rows + 1, 0:chan]

    loop(1, n_row, lambda d: col_copy(d, row).wait_send())
    loop(1, n_col, lambda d: row_copy(d, col).wait_send())
    for side in range(2):
        loop(0, n_row, lambda d: cedge_copy(side, d, row).wait_send())
        loop(0, n_col, lambda d: redge_copy(side, d, col).wait_send())
    loop(1, n_all, lambda d: rs_copy(d, (me + d) % n_all, me).wait_send())
    loop(1, n_all, lambda d: ag_copy(d, (me + d) % n_all, me).wait_send())


def solution(mesh):
    n_row, n_col, n_rep = (mesh.shape[axis] for axis in ("row", "col", "rep"))
    n_all = n_row * n_col * n_rep

    def per_device(
        emb_row,
        emb_col,
        proj_row,
        proj_col,
        pair_out,
        pair_bias,
        conv_weight,
        conv_bias,
        target,
        kept_tiles,
    ):
        chan, edge = target.shape[0], target.shape[1]
        rank = pair_out.shape[0]
        pairs = edge // 2
        used = 3 * chan + 3 * chan // 2 + 8
        chunk = 8 * pl.cdiv(used, 8 * n_all)

        def shared(proj, emb, axis):
            width = emb.shape[1]
            if width % 16 == 0:
                return proj
            return lax.dynamic_slice_in_dim(proj, lax.axis_index(axis) * width, width, 0)

        dma = pltpu.SemaphoreType.DMA
        vmem = pl.BlockSpec(memory_space=pltpu.VMEM)
        loss, grads, bias = pl.pallas_call(
            functools.partial(kernel, (n_row, n_col, n_rep, edge, chan, chunk)),
            out_shape=(
                jax.ShapeDtypeStruct((edge, edge), F32),
                jax.ShapeDtypeStruct((3, 3, chan, chan), F32),
                jax.ShapeDtypeStruct((1, chan), F32),
            ),
            in_specs=[vmem] * 9 + [pl.BlockSpec(memory_space=pltpu.SMEM)],
            out_specs=(vmem,) * 3,
            scratch_shapes=[
                pltpu.VMEM((n_col, edge + 16, rank), F32),
                pltpu.VMEM((2, n_col, 16, rank), F32),
                pltpu.VMEM((n_row, edge, rank), F32),
                pltpu.VMEM((2, n_row, 8, rank), F32),
                pltpu.VMEM((edge + 16, rank), F32),
                pltpu.VMEM((edge + 16, rank), F32),
                pltpu.VMEM((3 * edge, rank), BF16),
                pltpu.VMEM((chan * edge, edge), F32),
                pltpu.VMEM(((pairs + 2) * 3 * chan, 2 * edge), BF16),
                pltpu.VMEM(((pairs + 4) * chan, 2 * edge), F32),
                pltpu.VMEM(((pairs + 4) * chan, 2 * edge), BF16),
                pltpu.VMEM((3 * chan, 3 * chan), F32),
                pltpu.VMEM((3 * chan, 3 * chan), F32),
                pltpu.VMEM((chan, 2 * edge), F32),
                pltpu.VMEM((n_all * chunk, 128), F32),
                pltpu.VMEM((n_all, chunk, 128), F32),
                pltpu.VMEM((n_all * chunk, 128), F32),
                dma((n_col,)),
                dma((n_col,)),
                dma((2, n_col)),
                dma((2, n_col)),
                dma((n_row,)),
                dma((n_row,)),
                dma((2, n_row)),
                dma((2, n_row)),
                dma((n_all,)),
                dma((n_all,)),
                dma((n_all,)),
                dma((n_all,)),
            ],
            compiler_params=pltpu.CompilerParams(collective_id=0, has_side_effects=True),
            name="pair_step",
        )(
            emb_row,
            emb_col,
            shared(proj_row, emb_row, "col"),
            shared(proj_col, emb_col, "row"),
            pair_out,
            pair_bias.reshape(1, chan),
            conv_weight,
            conv_bias.reshape(1, chan),
            target,
            kept_tiles,
        )
        return loss, grads, bias.reshape(chan)

    in_specs = (
        P(("grp", "row", "rep"), "col"),
        P(("grp", "col"), "row"),
        P(),
        P(),
        P(),
        P(),
        P(),
        P(),
        P(None, ("grp", "row", "rep"), "col"),
        P(("grp", "row", "rep"), "col"),
    )
    out_specs = (P(("grp", "row", "rep"), "col"), P("grp", None, None, None), P("grp"))
    return jax.shard_map(
        per_device, mesh=mesh, in_specs=in_specs, out_specs=out_specs, check_vma=False
    )
```

```python
import functools

import jax
import jax.numpy as jnp
from jax import lax
from jax.experimental import pallas as pl
from jax.experimental.pallas import tpu as pltpu
from jax.sharding import PartitionSpec as P

MESH = pl.DeviceIdType.MESH
F32 = jnp.float32
BF16 = jnp.bfloat16
NT = (((1,), (1,)), ((), ()))


def loop(low, high, body):
    if high - low <= 16:
        for d in range(low, high):
            body(d)
    else:
        lax.fori_loop(low, high, lambda d, _: (body(d), 0)[1], 0)


def columns(ref, width, index, count):
    everything = ref.shape[1]
    if width % 128 == 0:
        return ref[:, pl.ds(pl.multiple_of(index * width, 128), width)]
    offset = max(i * width % 128 for i in range(count))
    window = min(-(-(offset + width) // 128) * 128, everything)
    tile = index * width // 128
    if any(i * width // 128 * 128 + window > everything for i in range(count)):
        tile = jnp.minimum(tile, (everything - window) // 128)
    value = ref[:, pl.ds(pl.multiple_of(tile * 128, 128), window)].astype(F32)
    shift = window - (index * width - tile * 128)
    return pltpu.roll(value, shift % window, 1)[:, 0:width].astype(BF16)


def kernel(
    sizes,
    emb_row,
    emb_col,
    proj_row,
    proj_col,
    pair_out,
    pair_bias,
    conv_weight,
    conv_bias,
    target,
    kept,
    loss_out,
    full,
    rowbuf,
    rowedge,
    colbuf,
    coledge,
    row_feat,
    col_wide,
    wide_t,
    target_in,
    target32,
    hid,
    base,
    grad_in,
    weight_f,
    total,
    bias_acc,
    part,
    reduced,
    target_sem,
    row_send,
    row_recv,
    redge_send,
    redge_recv,
    col_send,
    col_recv,
    cedge_send,
    cedge_recv,
    rs_send,
    rs_recv,
    ag_send,
    ag_recv,
):
    n_row, n_col, n_rep, edge, chan, chunk = sizes
    n_all = n_row * n_col * n_rep
    pairs = edge // 2
    row, col, rep = lax.axis_index("row"), lax.axis_index("col"), lax.axis_index("rep")
    line = row * n_rep + rep
    n_line = n_row * n_rep
    me = line * n_col + col

    def device(index):
        across = index % n_col
        along = index // n_col
        return {"row": along // n_rep, "rep": along % n_rep, "col": across}

    barrier = pltpu.get_barrier_semaphore()
    loop(
        1,
        n_all,
        lambda d: pl.semaphore_signal(
            barrier, inc=1, device_id=device((me + d) % n_all), device_id_type=MESH
        ),
    )

    fetch = pltpu.make_async_copy(target, target_in, target_sem)
    fetch.start()

    keep = kept[0, 0].astype(F32)
    part_row = lax.dot_general(
        emb_row[...],
        columns(proj_row, emb_row.shape[1], col, n_col),
        NT,
        preferred_element_type=F32,
    )
    part_col = jnp.dot(
        columns(proj_col, emb_col.shape[0], row, n_row),
        emb_col[...],
        preferred_element_type=F32,
    ).T
    rank = part_row.shape[1]
    rowbuf[col, 8 : edge + 8, :] = part_row
    rowbuf[col, 0:8, :] = jnp.full((8, rank), keep, F32)
    rowbuf[col, edge + 8 : edge + 16, :] = jnp.full((8, rank), keep, F32)
    colbuf[row, :, :] = part_col

    pl.semaphore_wait(barrier, n_all - 1)

    def row_copy(d, src):
        return pltpu.make_async_remote_copy(
            src_ref=rowbuf.at[src],
            dst_ref=rowbuf.at[src],
            send_sem=row_send.at[d],
            recv_sem=row_recv.at[src],
            device_id={"col": (col + d) % n_col},
            device_id_type=MESH,
        )

    def redge_copy(side, d, src):
        to = (line + (1 if side == 0 else n_line - 1)) % n_line
        return pltpu.make_async_remote_copy(
            src_ref=rowbuf.at[src, pl.ds(edge if side == 0 else 0, 16)],
            dst_ref=rowedge.at[side, src],
            send_sem=redge_send.at[side, d],
            recv_sem=redge_recv.at[side, src],
            device_id={"row": to // n_rep, "rep": to % n_rep, "col": (col + d) % n_col},
            device_id_type=MESH,
        )

    def col_copy(d, src):
        return pltpu.make_async_remote_copy(
            src_ref=colbuf.at[src],
            dst_ref=colbuf.at[src],
            send_sem=col_send.at[d],
            recv_sem=col_recv.at[src],
            device_id={"row": (row + d) % n_row},
            device_id_type=MESH,
        )

    def cedge_copy(side, d, src):
        to = (col + (1 if side == 0 else n_col - 1)) % n_col
        return pltpu.make_async_remote_copy(
            src_ref=colbuf.at[src, pl.ds(edge - 8 if side == 0 else 0, 8)],
            dst_ref=coledge.at[side, src],
            send_sem=cedge_send.at[side, d],
            recv_sem=cedge_recv.at[side, src],
            device_id={"row": (row + d) % n_row, "col": to},
            device_id_type=MESH,
        )

    loop(1, n_row, lambda d: col_copy(d, row).start())
    loop(1, n_col, lambda d: row_copy(d, col).start())
    for side in range(2):
        loop(0, n_row, lambda d: cedge_copy(side, d, row).start())
        loop(0, n_col, lambda d: redge_copy(side, d, col).start())

    fetch.wait()

    def widen(c, _):
        start = pl.multiple_of(c * edge, edge)
        target32[pl.ds(start, edge), :] = target_in[c].astype(F32)
        return 0

    lax.fori_loop(0, chan, widen, 0, unroll=4)
    for a in range(3):
        for b in range(3):
            weight_f[b * chan : (b + 1) * chan, a * chan : (a + 1) * chan] = conv_weight[
                a, b
            ].astype(F32)
    weight_t = weight_f[...].T.astype(BF16)
    out_t = pair_out[...].astype(F32).T
    pair_b = jnp.broadcast_to(pair_bias[...], (128, chan)).T
    conv_b = jnp.broadcast_to(conv_bias[...], (128, chan)).T
    zeros = jnp.zeros((2 * chan, 2 * edge), BF16)
    grad_in[0 : 2 * chan, :] = zeros
    grad_in[(pairs + 2) * chan : (pairs + 4) * chan, :] = zeros
    base[0 : 2 * chan, :] = zeros.astype(F32)
    base[(pairs + 2) * chan : (pairs + 4) * chan, :] = zeros.astype(F32)
    bias_acc[...] = jnp.zeros_like(bias_acc)
    total[...] = jnp.zeros_like(total)

    loop(1, n_row, lambda d: col_copy(d, (row + n_row - d) % n_row).wait_recv())
    loop(1, n_col, lambda d: row_copy(d, (col + n_col - d) % n_col).wait_recv())
    for side in range(2):
        loop(0, n_row, lambda d: cedge_copy(side, d, (row + n_row - d) % n_row).wait_recv())
        loop(0, n_col, lambda d: redge_copy(side, d, (col + n_col - d) % n_col).wait_recv())

    def rounded(x):
        return x.astype(BF16).astype(F32)

    row_feat[0:8, :] = rounded(sum(rowedge[0, c, 0:8, :] for c in range(n_col)))
    row_feat[8 : edge + 8, :] = rounded(sum(rowbuf[c, 8 : edge + 8, :] for c in range(n_col)))
    row_feat[edge + 8 : edge + 16, :] = rounded(
        sum(rowedge[1, c, 8:16, :] for c in range(n_col))
    )
    col_wide[0:8, :] = sum(coledge[0, r] for r in range(n_row))
    col_wide[8 : edge + 8, :] = sum(colbuf[r] for r in range(n_row))
    col_wide[edge + 8 : edge + 16, :] = sum(coledge[1, r] for r in range(n_row))
    for b in range(3):
        wide_t[b * edge : (b + 1) * edge, :] = col_wide[
            6 + 2 * b : 6 + 2 * b + edge, :
        ].astype(BF16)

    lane = lax.broadcasted_iota(jnp.int32, (1, edge), 1)
    before, after = (col + n_col - 1) % n_col, (col + 1) % n_col
    has_before = (col > 0).astype(F32)
    has_after = (col < n_col - 1).astype(F32)

    def masks(get, valid):
        here, left, right = (
            jnp.broadcast_to(get(c), (1, edge)) * scale
            for c, scale in ((col, valid), (before, valid * has_before), (after, valid * has_after))
        )
        return (jnp.where(lane < 2, left, here), here, jnp.where(lane >= edge - 2, right, here))

    top = masks(lambda c: rowedge[0, c, 8:9, 0:1], (line > 0).astype(F32))
    middle = masks(lambda c: rowbuf[c, 0:1, 0:1], jnp.float32(1))
    bottom = masks(lambda c: rowedge[1, c, 0:1, 0:1], (line < n_line - 1).astype(F32))

    def features(pair, count, mask, inner):
        scaled = []
        for r in range(2 * count):
            feat = row_feat[pl.ds(2 * pair + 8 + r, 1), :]
            scaled.append((out_t * feat).astype(BF16))
        product = lax.dot_general(
            jnp.concatenate(scaled, axis=0), wide_t[...], NT, preferred_element_type=F32
        )
        for r in range(2 * count):
            p = pair + r // 2
            lanes = slice((r % 2) * edge, (r % 2 + 1) * edge)
            for b in range(3):
                value = product[r * chan : (r + 1) * chan, b * edge : (b + 1) * edge] + pair_b
                start = pl.multiple_of((p + 1) * 3 * chan + b * chan, chan)
                hid[pl.ds(start, chan), lanes] = (jnp.maximum(value, 0.0) * mask[b]).astype(BF16)
                if inner and b == 1:
                    aim = target32[pl.ds(2 * pair + r, chan, stride=edge), :]
                    start = pl.multiple_of((p + 2) * chan, chan)
                    base[pl.ds(start, chan), lanes] = (value + conv_b) - aim

    features(-1, 1, top, False)
    features(pairs, 1, bottom, False)
    group = 4

    def feature_step(g, _):
        features(g * group, group, middle, True)
        return 0

    lax.fori_loop(0, pairs // group, feature_step, 0)

    def conv_of(p):
        start = pl.multiple_of((p + 1) * 3 * chan, 3 * chan)
        return jnp.dot(weight_t, hid[pl.ds(start, 3 * chan), :], preferred_element_type=F32)

    def slot(p):
        return pl.ds(pl.multiple_of((p + 2) * chan, chan), chan)

    def spread(p, done):
        y = conv_of(p)
        base[slot(p + 1), :] += y[0:chan]
        base[slot(p), :] += y[chan : 2 * chan]
        if done:
            differ = (base[slot(p - 1), :] + y[2 * chan :]) * keep
            grad_in[slot(p - 1), :] = differ.astype(BF16)
            bias_acc[...] += differ
            loss = 0.5 * jnp.sum(differ * differ, axis=0, keepdims=True)
            loss_out[pl.ds(2 * (p - 1), 1), :] = loss[:, 0:edge]
            loss_out[pl.ds(2 * (p - 1) + 1, 1), :] = loss[:, edge : 2 * edge]

    spread(-1, False)
    spread(0, False)

    def conv_step(g, _):
        for r in range(4):
            spread(1 + g * 4 + r, True)
        return 0

    lax.fori_loop(0, pairs // 4, conv_step, 0)

    def grad_step(g, _):
        value = total[...]
        for r in range(6):
            p = g * 6 + r - 1
            start = pl.multiple_of((p + 1) * 3 * chan, 3 * chan)
            near = pl.multiple_of((p + 1) * chan, chan)
            value = value + lax.dot_general(
                hid[pl.ds(start, 3 * chan), :],
                grad_in[pl.ds(near, 3 * chan), :],
                NT,
                preferred_element_type=F32,
            )
        total[...] = value
        return 0

    lax.fori_loop(0, (pairs + 2) // 6, grad_step, 0)

    norm = 1.0 / (edge * edge)
    half = 3 * chan // 2
    rows = 3 * chan + half
    sums = total[...] * norm
    flat = jnp.concatenate(
        [
            sums[:, 0 : 2 * chan],
            jnp.concatenate([sums[0:half, 2 * chan :], sums[half:, 2 * chan :]], axis=1),
        ],
        axis=0,
    )
    bias_sum = lax.dot_general(
        jnp.ones((8, 2 * edge), F32),
        bias_acc[...] * norm,
        NT,
        precision=lax.Precision.HIGHEST,
        preferred_element_type=F32,
    )
    part[0:rows, :] = flat
    part[rows : rows + 8, :] = jnp.concatenate([bias_sum, bias_sum], axis=1)
    rest = n_all * chunk - rows - 8
    if rest > 0:
        part[rows + 8 :, :] = jnp.zeros((rest, 128), F32)

    def piece(index):
        return pl.ds(pl.multiple_of(index * chunk, 8), chunk)

    def rs_copy(d, to, src):
        return pltpu.make_async_remote_copy(
            src_ref=part.at[piece(to)],
            dst_ref=reduced.at[src],
            send_sem=rs_send.at[d],
            recv_sem=rs_recv.at[src],
            device_id=device(to),
            device_id_type=MESH,
        )

    def ag_copy(d, to, src):
        return pltpu.make_async_remote_copy(
            src_ref=full.at[piece(src)],
            dst_ref=full.at[piece(src)],
            send_sem=ag_send.at[d],
            recv_sem=ag_recv.at[src],
            device_id=device(to),
            device_id_type=MESH,
        )

    loop(1, n_all, lambda d: rs_copy(d, (me + d) % n_all, me).start())
    reduced[me] = part[piece(me), :]
    loop(1, n_all, lambda d: rs_copy(d, (me + d) % n_all, (me + n_all - d) % n_all).wait_recv())
    if n_all <= 16:
        own = sum(reduced[r] for r in range(n_all))
    else:
        own = lax.fori_loop(
            0, n_all, lambda r, x: x + reduced[r], jnp.zeros((chunk, 128), F32)
        )
    full[piece(me), :] = own
    loop(1, n_all, lambda d: ag_copy(d, (me + d) % n_all, me).start())
    loop(1, n_all, lambda d: ag_copy(d, (me + d) % n_all, (me + n_all - d) % n_all).wait_recv())

    loop(1, n_row, lambda d: col_copy(d, row).wait_send())
    loop(1, n_col, lambda d: row_copy(d, col).wait_send())
    for side in range(2):
        loop(0, n_row, lambda d: cedge_copy(side, d, row).wait_send())
        loop(0, n_col, lambda d: redge_copy(side, d, col).wait_send())
    loop(1, n_all, lambda d: rs_copy(d, (me + d) % n_all, me).wait_send())
    loop(1, n_all, lambda d: ag_copy(d, (me + d) % n_all, me).wait_send())


def finish(loss_in, full, loss_out, conv_grad_out, bias_out):
    chan = bias_out.shape[1]
    half = 3 * chan // 2
    rows = 3 * chan + half
    loss_out[...] = loss_in[...]
    for b in range(3):
        low = b * chan
        conv_grad_out[2, b] = full[low : low + chan, 0:chan]
        conv_grad_out[1, b] = full[low : low + chan, chan : 2 * chan]
    low = 3 * chan
    conv_grad_out[0, 0] = full[low : low + chan, 0:chan]
    conv_grad_out[0, 1, 0 : half - chan] = full[low + chan : low + half, 0:chan]
    conv_grad_out[0, 1, half - chan :] = full[low : low + 2 * chan - half, chan : 2 * chan]
    conv_grad_out[0, 2] = full[low + 2 * chan - half : low + half, chan : 2 * chan]
    bias_out[...] = full[rows : rows + 1, 0:chan]


def solution(mesh):
    n_row, n_col, n_rep = (mesh.shape[axis] for axis in ("row", "col", "rep"))
    n_all = n_row * n_col * n_rep

    def per_device(
        emb_row,
        emb_col,
        proj_row,
        proj_col,
        pair_out,
        pair_bias,
        conv_weight,
        conv_bias,
        target,
        kept_tiles,
    ):
        chan, edge = target.shape[0], target.shape[1]
        rank = pair_out.shape[0]
        pairs = edge // 2
        used = 3 * chan + 3 * chan // 2 + 8
        chunk = 8 * pl.cdiv(used, 8 * n_all)

        dma = pltpu.SemaphoreType.DMA
        vmem = pl.BlockSpec(memory_space=pltpu.VMEM)
        loss, sums = pl.pallas_call(
            functools.partial(kernel, (n_row, n_col, n_rep, edge, chan, chunk)),
            out_shape=(
                jax.ShapeDtypeStruct((edge, edge), F32),
                jax.ShapeDtypeStruct((n_all * chunk, 128), F32),
            ),
            in_specs=[vmem] * 8
            + [pl.BlockSpec(memory_space=pl.ANY), pl.BlockSpec(memory_space=pltpu.SMEM)],
            out_specs=(vmem,) * 2,
            scratch_shapes=[
                pltpu.VMEM((n_col, edge + 16, rank), F32),
                pltpu.VMEM((2, n_col, 16, rank), F32),
                pltpu.VMEM((n_row, edge, rank), F32),
                pltpu.VMEM((2, n_row, 8, rank), F32),
                pltpu.VMEM((edge + 16, rank), F32),
                pltpu.VMEM((edge + 16, rank), F32),
                pltpu.VMEM((3 * edge, rank), BF16),
                pltpu.VMEM((chan, edge, edge), BF16),
                pltpu.VMEM((chan * edge, edge), F32),
                pltpu.VMEM(((pairs + 2) * 3 * chan, 2 * edge), BF16),
                pltpu.VMEM(((pairs + 4) * chan, 2 * edge), F32),
                pltpu.VMEM(((pairs + 4) * chan, 2 * edge), BF16),
                pltpu.VMEM((3 * chan, 3 * chan), F32),
                pltpu.VMEM((3 * chan, 3 * chan), F32),
                pltpu.VMEM((chan, 2 * edge), F32),
                pltpu.VMEM((n_all * chunk, 128), F32),
                pltpu.VMEM((n_all, chunk, 128), F32),
                pltpu.SemaphoreType.DMA,
                dma((n_col,)),
                dma((n_col,)),
                dma((2, n_col)),
                dma((2, n_col)),
                dma((n_row,)),
                dma((n_row,)),
                dma((2, n_row)),
                dma((2, n_row)),
                dma((n_all,)),
                dma((n_all,)),
                dma((n_all,)),
                dma((n_all,)),
            ],
            compiler_params=pltpu.CompilerParams(collective_id=0, has_side_effects=True),
            name="pair_step",
        )(
            emb_row,
            emb_col.T,
            proj_row.T,
            proj_col.T,
            pair_out,
            pair_bias.reshape(1, chan),
            conv_weight,
            conv_bias.reshape(1, chan),
            target,
            kept_tiles,
        )
        loss, grads, bias = pl.pallas_call(
            finish,
            out_shape=(
                jax.ShapeDtypeStruct((edge, edge), F32),
                jax.ShapeDtypeStruct((3, 3, chan, chan), F32),
                jax.ShapeDtypeStruct((1, chan), F32),
            ),
            in_specs=[vmem] * 2,
            out_specs=(vmem,) * 3,
            name="finish",
        )(loss, sums)
        return loss, grads, bias.reshape(chan)

    in_specs = (
        P(("grp", "row", "rep"), "col"),
        P(("grp", "col"), "row"),
        P(),
        P(),
        P(),
        P(),
        P(),
        P(),
        P(None, ("grp", "row", "rep"), "col"),
        P(("grp", "row", "rep"), "col"),
    )
    out_specs = (P(("grp", "row", "rep"), "col"), P("grp", None, None, None), P("grp"))
    return jax.shard_map(
        per_device, mesh=mesh, in_specs=in_specs, out_specs=out_specs, check_vma=False
    )
```

```python
import functools

import jax
import jax.numpy as jnp
from jax import lax
from jax.experimental import pallas as pl
from jax.experimental.pallas import tpu as pltpu
from jax.sharding import PartitionSpec as P

MESH = pl.DeviceIdType.MESH
F32 = jnp.float32
BF16 = jnp.bfloat16
NT = (((1,), (1,)), ((), ()))


def loop(low, high, body):
    if high - low <= 16:
        for d in range(low, high):
            body(d)
    else:
        lax.fori_loop(low, high, lambda d, _: (body(d), 0)[1], 0)


def columns(ref, width, index, count):
    everything = ref.shape[1]
    if width % 128 == 0:
        return ref[:, pl.ds(pl.multiple_of(index * width, 128), width)]
    offset = max(i * width % 128 for i in range(count))
    window = min(-(-(offset + width) // 128) * 128, everything)
    tile = index * width // 128
    if any(i * width // 128 * 128 + window > everything for i in range(count)):
        tile = jnp.minimum(tile, (everything - window) // 128)
    value = ref[:, pl.ds(pl.multiple_of(tile * 128, 128), window)].astype(F32)
    shift = window - (index * width - tile * 128)
    return pltpu.roll(value, shift % window, 1)[:, 0:width].astype(BF16)


def kernel(
    sizes,
    emb_row_hbm,
    emb_col_hbm,
    proj_row_hbm,
    proj_col_hbm,
    pair_out,
    pair_bias,
    conv_weight_hbm,
    conv_bias,
    target,
    kept,
    loss_out,
    full,
    emb_row,
    emb_col,
    proj_row,
    proj_col,
    conv_weight,
    in_sem,
    rowtail,
    coltail,
    rowbuf,
    rowedge,
    colbuf,
    coledge,
    row_feat,
    col_wide,
    wide_t,
    target_in,
    target32,
    hid,
    base,
    grad_in,
    weight_f,
    total,
    bias_acc,
    part,
    reduced,
    target_sem,
    row_send,
    row_recv,
    redge_send,
    redge_recv,
    col_send,
    col_recv,
    cedge_send,
    cedge_recv,
    rs_send,
    rs_recv,
    ag_send,
    ag_recv,
):
    n_row, n_col, n_rep, edge, chan, chunk = sizes
    n_all = n_row * n_col * n_rep
    pairs = edge // 2
    row, col, rep = lax.axis_index("row"), lax.axis_index("col"), lax.axis_index("rep")
    line = row * n_rep + rep
    n_line = n_row * n_rep
    me = line * n_col + col

    def device(index):
        across = index % n_col
        along = index // n_col
        return {"row": along // n_rep, "rep": along % n_rep, "col": across}

    barrier = pltpu.get_barrier_semaphore()
    loop(
        1,
        n_all,
        lambda d: pl.semaphore_signal(
            barrier, inc=1, device_id=device((me + d) % n_all), device_id_type=MESH
        ),
    )

    inputs = [
        pltpu.make_async_copy(src, dst, in_sem.at[i])
        for i, (src, dst) in enumerate(
            (
                (emb_row_hbm, emb_row),
                (proj_row_hbm, proj_row),
                (emb_col_hbm, emb_col),
                (proj_col_hbm, proj_col),
                (conv_weight_hbm, conv_weight),
            )
        )
    ]
    for copy in inputs:
        copy.start()
    fetch = pltpu.make_async_copy(target, target_in, target_sem)
    fetch.start()

    def rounded(x):
        return x.astype(BF16).astype(F32)

    keep = kept[0, 0].astype(F32)
    for copy in inputs[2:4]:
        copy.wait()
    part_col = jnp.dot(
        columns(proj_col, emb_col.shape[0], row, n_row),
        emb_col[...],
        preferred_element_type=F32,
    )
    for copy in inputs[0:2]:
        copy.wait()
    part_row = lax.dot_general(
        columns(proj_row, emb_row.shape[1], col, n_col),
        emb_row[...],
        NT,
        preferred_element_type=F32,
    )
    rank = part_row.shape[0]
    colbuf[row] = part_col.astype(BF16)
    rowbuf[col, 0:rank, :] = part_row.astype(BF16)
    rowbuf[col, rank:, :] = jnp.full((16, edge), keep, F32).astype(BF16)
    turned = rounded(part_col).T
    coltail[0] = turned[edge - 8 :]
    coltail[1] = turned[0:8]
    turned = rounded(part_row).T
    rowtail[0, 0:8] = turned[edge - 8 :]
    rowtail[1, 0:8] = turned[0:8]
    for side in range(2):
        rowtail[side, 8:16] = jnp.full((8, rank), keep, F32)

    pl.semaphore_wait(barrier, n_all - 1)

    def row_copy(d, src):
        return pltpu.make_async_remote_copy(
            src_ref=rowbuf.at[src],
            dst_ref=rowbuf.at[src],
            send_sem=row_send.at[d],
            recv_sem=row_recv.at[src],
            device_id={"col": (col + d) % n_col},
            device_id_type=MESH,
        )

    def redge_copy(side, d, src):
        to = (line + (1 if side == 0 else n_line - 1)) % n_line
        return pltpu.make_async_remote_copy(
            src_ref=rowtail.at[side],
            dst_ref=rowedge.at[side, src],
            send_sem=redge_send.at[side, d],
            recv_sem=redge_recv.at[side, src],
            device_id={"row": to // n_rep, "rep": to % n_rep, "col": (col + d) % n_col},
            device_id_type=MESH,
        )

    def col_copy(d, src):
        return pltpu.make_async_remote_copy(
            src_ref=colbuf.at[src],
            dst_ref=colbuf.at[src],
            send_sem=col_send.at[d],
            recv_sem=col_recv.at[src],
            device_id={"row": (row + d) % n_row},
            device_id_type=MESH,
        )

    def cedge_copy(side, d, src):
        to = (col + (1 if side == 0 else n_col - 1)) % n_col
        return pltpu.make_async_remote_copy(
            src_ref=coltail.at[side],
            dst_ref=coledge.at[side, src],
            send_sem=cedge_send.at[side, d],
            recv_sem=cedge_recv.at[side, src],
            device_id={"row": (row + d) % n_row, "col": to},
            device_id_type=MESH,
        )

    loop(1, n_row, lambda d: col_copy(d, row).start())
    loop(1, n_col, lambda d: row_copy(d, col).start())
    for side in range(2):
        loop(0, n_row, lambda d: cedge_copy(side, d, row).start())
        loop(0, n_col, lambda d: redge_copy(side, d, col).start())

    fetch.wait()
    inputs[4].wait()

    def widen(c, _):
        start = pl.multiple_of(c * edge, edge)
        target32[pl.ds(start, edge), :] = target_in[c].astype(F32)
        return 0

    lax.fori_loop(0, chan, widen, 0, unroll=4)
    for a in range(3):
        for b in range(3):
            weight_f[b * chan : (b + 1) * chan, a * chan : (a + 1) * chan] = conv_weight[
                a, b
            ].astype(F32)
    weight_t = weight_f[...].T.astype(BF16)
    out_t = pair_out[...].astype(F32).T
    pair_b = jnp.broadcast_to(pair_bias[...], (128, chan)).T
    conv_b = jnp.broadcast_to(conv_bias[...], (128, chan)).T
    zeros = jnp.zeros((2 * chan, 2 * edge), BF16)
    grad_in[0 : 2 * chan, :] = zeros
    grad_in[(pairs + 2) * chan : (pairs + 4) * chan, :] = zeros
    base[0 : 2 * chan, :] = zeros.astype(F32)
    base[(pairs + 2) * chan : (pairs + 4) * chan, :] = zeros.astype(F32)
    bias_acc[...] = jnp.zeros_like(bias_acc)
    total[...] = jnp.zeros_like(total)

    loop(1, n_row, lambda d: col_copy(d, (row + n_row - d) % n_row).wait_recv())
    loop(1, n_col, lambda d: row_copy(d, (col + n_col - d) % n_col).wait_recv())
    for side in range(2):
        loop(0, n_row, lambda d: cedge_copy(side, d, (row + n_row - d) % n_row).wait_recv())
        loop(0, n_col, lambda d: redge_copy(side, d, (col + n_col - d) % n_col).wait_recv())

    def summed(terms):
        return sum(x.astype(F32) for x in terms)

    row_feat[0:8, :] = rounded(summed(rowedge[0, c, 0:8, :] for c in range(n_col)))
    row_feat[8 : edge + 8, :] = rounded(summed(rowbuf[c, 0:rank, :] for c in range(n_col))).T
    row_feat[edge + 8 :, :] = rounded(summed(rowedge[1, c, 0:8, :] for c in range(n_col)))
    col_wide[0:8, :] = summed(coledge[0, r] for r in range(n_row))
    col_wide[8 : edge + 8, :] = summed(colbuf[r] for r in range(n_row)).T
    col_wide[edge + 8 :, :] = summed(coledge[1, r] for r in range(n_row))
    for b in range(3):
        wide_t[b * edge : (b + 1) * edge, :] = col_wide[
            6 + 2 * b : 6 + 2 * b + edge, :
        ].astype(BF16)

    lane = lax.broadcasted_iota(jnp.int32, (1, edge), 1)
    before, after = (col + n_col - 1) % n_col, (col + 1) % n_col
    has_before = (col > 0).astype(F32)
    has_after = (col < n_col - 1).astype(F32)

    def masks(get, valid):
        here, left, right = (
            jnp.broadcast_to(get(c), (1, edge)) * scale
            for c, scale in ((col, valid), (before, valid * has_before), (after, valid * has_after))
        )
        return (jnp.where(lane < 2, left, here), here, jnp.where(lane >= edge - 2, right, here))

    top = masks(lambda c: rowedge[0, c, 8:9, 0:1], (line > 0).astype(F32))
    middle = masks(lambda c: rowbuf[c, rank:, 0:1].astype(F32)[0:1], jnp.float32(1))
    bottom = masks(lambda c: rowedge[1, c, 8:9, 0:1], (line < n_line - 1).astype(F32))

    def features(pair, count, mask, inner):
        scaled = []
        for r in range(2 * count):
            feat = row_feat[pl.ds(2 * pair + 8 + r, 1), :]
            scaled.append((out_t * feat).astype(BF16))
        product = lax.dot_general(
            jnp.concatenate(scaled, axis=0), wide_t[...], NT, preferred_element_type=F32
        )
        for r in range(2 * count):
            p = pair + r // 2
            lanes = slice((r % 2) * edge, (r % 2 + 1) * edge)
            for b in range(3):
                value = product[r * chan : (r + 1) * chan, b * edge : (b + 1) * edge] + pair_b
                start = pl.multiple_of((p + 1) * 3 * chan + b * chan, chan)
                hid[pl.ds(start, chan), lanes] = (jnp.maximum(value, 0.0) * mask[b]).astype(BF16)
                if inner and b == 1:
                    aim = target32[pl.ds(2 * pair + r, chan, stride=edge), :]
                    start = pl.multiple_of((p + 2) * chan, chan)
                    base[pl.ds(start, chan), lanes] = (value + conv_b) - aim

    features(-1, 1, top, False)
    features(pairs, 1, bottom, False)
    group = 4

    def feature_step(g, _):
        features(g * group, group, middle, True)
        return 0

    lax.fori_loop(0, pairs // group, feature_step, 0)

    def conv_of(p):
        start = pl.multiple_of((p + 1) * 3 * chan, 3 * chan)
        return jnp.dot(weight_t, hid[pl.ds(start, 3 * chan), :], preferred_element_type=F32)

    def slot(p):
        return pl.ds(pl.multiple_of((p + 2) * chan, chan), chan)

    def spread(p, done):
        y = conv_of(p)
        base[slot(p + 1), :] += y[0:chan]
        base[slot(p), :] += y[chan : 2 * chan]
        if done:
            differ = (base[slot(p - 1), :] + y[2 * chan :]) * keep
            grad_in[slot(p - 1), :] = differ.astype(BF16)
            bias_acc[...] += differ
            loss = 0.5 * jnp.sum(differ * differ, axis=0, keepdims=True)
            loss_out[pl.ds(2 * (p - 1), 1), :] = loss[:, 0:edge]
            loss_out[pl.ds(2 * (p - 1) + 1, 1), :] = loss[:, edge : 2 * edge]

    spread(-1, False)
    spread(0, False)

    def conv_step(g, _):
        for r in range(4):
            spread(1 + g * 4 + r, True)
        return 0

    lax.fori_loop(0, pairs // 4, conv_step, 0)

    def grad_step(g, _):
        value = total[...]
        for r in range(6):
            p = g * 6 + r - 1
            start = pl.multiple_of((p + 1) * 3 * chan, 3 * chan)
            near = pl.multiple_of((p + 1) * chan, chan)
            value = value + lax.dot_general(
                hid[pl.ds(start, 3 * chan), :],
                grad_in[pl.ds(near, 3 * chan), :],
                NT,
                preferred_element_type=F32,
            )
        total[...] = value
        return 0

    lax.fori_loop(0, (pairs + 2) // 6, grad_step, 0)

    norm = 1.0 / (edge * edge)
    half = 3 * chan // 2
    rows = 3 * chan + half
    sums = total[...] * norm
    flat = jnp.concatenate(
        [
            sums[:, 0 : 2 * chan],
            jnp.concatenate([sums[0:half, 2 * chan :], sums[half:, 2 * chan :]], axis=1),
        ],
        axis=0,
    )
    bias_sum = lax.dot_general(
        jnp.ones((8, 2 * edge), F32),
        bias_acc[...] * norm,
        NT,
        precision=lax.Precision.HIGHEST,
        preferred_element_type=F32,
    )
    part[0:rows, :] = flat
    part[rows : rows + 8, :] = jnp.concatenate([bias_sum, bias_sum], axis=1)
    rest = n_all * chunk - rows - 8
    if rest > 0:
        part[rows + 8 :, :] = jnp.zeros((rest, 128), F32)

    def piece(index):
        return pl.ds(pl.multiple_of(index * chunk, 8), chunk)

    def rs_copy(d, to, src):
        return pltpu.make_async_remote_copy(
            src_ref=part.at[piece(to)],
            dst_ref=reduced.at[src],
            send_sem=rs_send.at[d],
            recv_sem=rs_recv.at[src],
            device_id=device(to),
            device_id_type=MESH,
        )

    def ag_copy(d, to, src):
        return pltpu.make_async_remote_copy(
            src_ref=full.at[src],
            dst_ref=full.at[src],
            send_sem=ag_send.at[d],
            recv_sem=ag_recv.at[src],
            device_id=device(to),
            device_id_type=MESH,
        )

    loop(1, n_all, lambda d: rs_copy(d, (me + d) % n_all, me).start())
    reduced[me] = part[piece(me), :]
    loop(1, n_all, lambda d: rs_copy(d, (me + d) % n_all, (me + n_all - d) % n_all).wait_recv())
    if n_all <= 16:
        own = sum(reduced[r] for r in range(n_all))
    else:
        own = lax.fori_loop(
            0, n_all, lambda r, x: x + reduced[r], jnp.zeros((chunk, 128), F32)
        )
    full[me] = own.astype(BF16)
    loop(1, n_all, lambda d: ag_copy(d, (me + d) % n_all, me).start())
    loop(1, n_all, lambda d: ag_copy(d, (me + d) % n_all, (me + n_all - d) % n_all).wait_recv())

    loop(1, n_row, lambda d: col_copy(d, row).wait_send())
    loop(1, n_col, lambda d: row_copy(d, col).wait_send())
    for side in range(2):
        loop(0, n_row, lambda d: cedge_copy(side, d, row).wait_send())
        loop(0, n_col, lambda d: redge_copy(side, d, col).wait_send())
    loop(1, n_all, lambda d: rs_copy(d, (me + d) % n_all, me).wait_send())
    loop(1, n_all, lambda d: ag_copy(d, (me + d) % n_all, me).wait_send())


def finish(loss_in, gathered, loss_out, conv_grad_out, bias_out, full):
    n_all, chunk = gathered.shape[0:2]

    def place(r):
        full[pl.ds(r * chunk, chunk), :] = gathered[r].astype(F32)

    loop(0, n_all, place)
    chan = bias_out.shape[1]
    half = 3 * chan // 2
    rows = 3 * chan + half
    loss_out[...] = loss_in[...]
    for b in range(3):
        low = b * chan
        conv_grad_out[2, b] = full[low : low + chan, 0:chan]
        conv_grad_out[1, b] = full[low : low + chan, chan : 2 * chan]
    low = 3 * chan
    conv_grad_out[0, 0] = full[low : low + chan, 0:chan]
    conv_grad_out[0, 1, 0 : half - chan] = full[low + chan : low + half, 0:chan]
    conv_grad_out[0, 1, half - chan :] = full[low : low + 2 * chan - half, chan : 2 * chan]
    conv_grad_out[0, 2] = full[low + 2 * chan - half : low + half, chan : 2 * chan]
    bias_out[...] = full[rows : rows + 1, 0:chan]


def solution(mesh):
    n_row, n_col, n_rep = (mesh.shape[axis] for axis in ("row", "col", "rep"))
    n_all = n_row * n_col * n_rep

    def per_device(
        emb_row,
        emb_col,
        proj_row,
        proj_col,
        pair_out,
        pair_bias,
        conv_weight,
        conv_bias,
        target,
        kept_tiles,
    ):
        chan, edge = target.shape[0], target.shape[1]
        rank = pair_out.shape[0]
        pairs = edge // 2
        used = 3 * chan + 3 * chan // 2 + 8
        chunk = 8 * pl.cdiv(used, 8 * n_all)

        dma = pltpu.SemaphoreType.DMA
        vmem = pl.BlockSpec(memory_space=pltpu.VMEM)
        hbm = pl.BlockSpec(memory_space=pl.ANY)
        loss, sums = pl.pallas_call(
            functools.partial(kernel, (n_row, n_col, n_rep, edge, chan, chunk)),
            out_shape=(
                jax.ShapeDtypeStruct((edge, edge), F32),
                jax.ShapeDtypeStruct((n_all, chunk, 128), BF16),
            ),
            in_specs=[hbm] * 4
            + [vmem] * 2
            + [hbm, vmem, hbm, pl.BlockSpec(memory_space=pltpu.SMEM)],
            out_specs=(vmem,) * 2,
            scratch_shapes=[
                pltpu.VMEM(emb_row.shape, BF16),
                pltpu.VMEM(emb_col.shape[::-1], BF16),
                pltpu.VMEM(proj_row.shape[::-1], BF16),
                pltpu.VMEM(proj_col.shape[::-1], BF16),
                pltpu.VMEM(conv_weight.shape, BF16),
                dma((5,)),
                pltpu.VMEM((2, 16, rank), F32),
                pltpu.VMEM((2, 8, rank), F32),
                pltpu.VMEM((n_col, rank + 16, edge), BF16),
                pltpu.VMEM((2, n_col, 16, rank), F32),
                pltpu.VMEM((n_row, rank, edge), BF16),
                pltpu.VMEM((2, n_row, 8, rank), F32),
                pltpu.VMEM((edge + 16, rank), F32),
                pltpu.VMEM((edge + 16, rank), F32),
                pltpu.VMEM((3 * edge, rank), BF16),
                pltpu.VMEM((chan, edge, edge), BF16),
                pltpu.VMEM((chan * edge, edge), F32),
                pltpu.VMEM(((pairs + 2) * 3 * chan, 2 * edge), BF16),
                pltpu.VMEM(((pairs + 4) * chan, 2 * edge), F32),
                pltpu.VMEM(((pairs + 4) * chan, 2 * edge), BF16),
                pltpu.VMEM((3 * chan, 3 * chan), F32),
                pltpu.VMEM((3 * chan, 3 * chan), F32),
                pltpu.VMEM((chan, 2 * edge), F32),
                pltpu.VMEM((n_all * chunk, 128), F32),
                pltpu.VMEM((n_all, chunk, 128), F32),
                pltpu.SemaphoreType.DMA,
                dma((n_col,)),
                dma((n_col,)),
                dma((2, n_col)),
                dma((2, n_col)),
                dma((n_row,)),
                dma((n_row,)),
                dma((2, n_row)),
                dma((2, n_row)),
                dma((n_all,)),
                dma((n_all,)),
                dma((n_all,)),
                dma((n_all,)),
            ],
            compiler_params=pltpu.CompilerParams(collective_id=0, has_side_effects=True),
            name="pair_step",
        )(
            emb_row,
            emb_col.T,
            proj_row.T,
            proj_col.T,
            pair_out,
            pair_bias.reshape(1, chan),
            conv_weight,
            conv_bias.reshape(1, chan),
            target,
            kept_tiles,
        )
        loss, grads, bias = pl.pallas_call(
            finish,
            out_shape=(
                jax.ShapeDtypeStruct((edge, edge), F32),
                jax.ShapeDtypeStruct((3, 3, chan, chan), F32),
                jax.ShapeDtypeStruct((1, chan), F32),
            ),
            in_specs=[vmem] * 2,
            out_specs=(vmem,) * 3,
            scratch_shapes=[pltpu.VMEM((n_all * chunk, 128), F32)],
            name="finish",
        )(loss, sums)
        return loss, grads, bias.reshape(chan)

    in_specs = (
        P(("grp", "row", "rep"), "col"),
        P(("grp", "col"), "row"),
        P(),
        P(),
        P(),
        P(),
        P(),
        P(),
        P(None, ("grp", "row", "rep"), "col"),
        P(("grp", "row", "rep"), "col"),
    )
    out_specs = (P(("grp", "row", "rep"), "col"), P("grp", None, None, None), P("grp"))
    return jax.shard_map(
        per_device, mesh=mesh, in_specs=in_specs, out_specs=out_specs, check_vma=False
    )
```

```python
import functools

import jax
import jax.numpy as jnp
from jax import lax
from jax.experimental import pallas as pl
from jax.experimental.pallas import tpu as pltpu
from jax.sharding import PartitionSpec as P

MESH = pl.DeviceIdType.MESH
F32 = jnp.float32
BF16 = jnp.bfloat16
NT = (((1,), (1,)), ((), ()))


def loop(low, high, body):
    if high - low <= 16:
        for d in range(low, high):
            body(d)
    else:
        lax.fori_loop(low, high, lambda d, _: (body(d), 0)[1], 0)


def columns(ref, width, index, count):
    everything = ref.shape[1]
    if width % 128 == 0:
        return ref[:, pl.ds(pl.multiple_of(index * width, 128), width)]
    offset = max(i * width % 128 for i in range(count))
    window = min(-(-(offset + width) // 128) * 128, everything)
    tile = index * width // 128
    if any(i * width // 128 * 128 + window > everything for i in range(count)):
        tile = jnp.minimum(tile, (everything - window) // 128)
    value = ref[:, pl.ds(pl.multiple_of(tile * 128, 128), window)].astype(F32)
    shift = window - (index * width - tile * 128)
    return pltpu.roll(value, shift % window, 1)[:, 0:width].astype(BF16)


def kernel(
    sizes,
    emb_row_hbm,
    emb_col_hbm,
    proj_row_hbm,
    proj_col_hbm,
    pair_out,
    pair_bias,
    conv_weight_hbm,
    conv_bias,
    target,
    kept,
    loss_out,
    full,
    emb_row,
    emb_col,
    proj_row,
    proj_col,
    conv_weight,
    in_sem,
    rowtail,
    coltail,
    rowbuf,
    rowedge,
    colbuf,
    coledge,
    row_feat,
    col_wide,
    wide_t,
    target_in,
    target32,
    hid,
    base,
    grad_in,
    weight_f,
    total,
    bias_acc,
    part,
    reduced,
    target_sem,
    row_send,
    row_recv,
    redge_send,
    redge_recv,
    col_send,
    col_recv,
    cedge_send,
    cedge_recv,
    rs_send,
    rs_recv,
    ag_send,
    ag_recv,
):
    n_row, n_col, n_rep, edge, chan, chunk = sizes
    n_all = n_row * n_col * n_rep
    pairs = edge // 2
    row, col, rep = lax.axis_index("row"), lax.axis_index("col"), lax.axis_index("rep")
    line = row * n_rep + rep
    n_line = n_row * n_rep
    me = line * n_col + col

    def device(index):
        across = index % n_col
        along = index // n_col
        return {"row": along // n_rep, "rep": along % n_rep, "col": across}

    barrier = pltpu.get_barrier_semaphore()
    loop(
        1,
        n_all,
        lambda d: pl.semaphore_signal(
            barrier, inc=1, device_id=device((me + d) % n_all), device_id_type=MESH
        ),
    )

    inputs = [
        pltpu.make_async_copy(src, dst, in_sem.at[i])
        for i, (src, dst) in enumerate(
            (
                (emb_row_hbm, emb_row),
                (proj_row_hbm, proj_row),
                (emb_col_hbm, emb_col),
                (proj_col_hbm, proj_col),
                (conv_weight_hbm, conv_weight),
            )
        )
    ]
    for copy in inputs:
        copy.start()
    fetch = pltpu.make_async_copy(target, target_in, target_sem)
    fetch.start()

    def rounded(x):
        return x.astype(BF16).astype(F32)

    keep = kept[0, 0].astype(F32)
    for copy in inputs[2:4]:
        copy.wait()
    part_col = jnp.dot(
        columns(proj_col, emb_col.shape[0], row, n_row),
        emb_col[...],
        preferred_element_type=F32,
    )
    for copy in inputs[0:2]:
        copy.wait()
    part_row = lax.dot_general(
        columns(proj_row, emb_row.shape[1], col, n_col),
        emb_row[...],
        NT,
        preferred_element_type=F32,
    )
    rank = part_row.shape[0]
    colbuf[row] = part_col.astype(BF16)
    rowbuf[col, 0:rank, :] = part_row.astype(BF16)
    rowbuf[col, rank:, :] = jnp.full((16, edge), keep, F32).astype(BF16)
    turned = rounded(part_col).T
    coltail[0] = turned[edge - 8 :]
    coltail[1] = turned[0:8]
    turned = rounded(part_row).T
    rowtail[0, 0:8] = turned[edge - 8 :]
    rowtail[1, 0:8] = turned[0:8]
    for side in range(2):
        rowtail[side, 8:16] = jnp.full((8, rank), keep, F32)

    pl.semaphore_wait(barrier, n_all - 1)

    def row_copy(d, src):
        return pltpu.make_async_remote_copy(
            src_ref=rowbuf.at[src],
            dst_ref=rowbuf.at[src],
            send_sem=row_send.at[d],
            recv_sem=row_recv.at[src],
            device_id={"col": (col + d) % n_col},
            device_id_type=MESH,
        )

    def redge_copy(side, d, src):
        to = (line + (1 if side == 0 else n_line - 1)) % n_line
        return pltpu.make_async_remote_copy(
            src_ref=rowtail.at[side],
            dst_ref=rowedge.at[side, src],
            send_sem=redge_send.at[side, d],
            recv_sem=redge_recv.at[side, src],
            device_id={"row": to // n_rep, "rep": to % n_rep, "col": (col + d) % n_col},
            device_id_type=MESH,
        )

    def col_copy(d, src):
        return pltpu.make_async_remote_copy(
            src_ref=colbuf.at[src],
            dst_ref=colbuf.at[src],
            send_sem=col_send.at[d],
            recv_sem=col_recv.at[src],
            device_id={"row": (row + d) % n_row},
            device_id_type=MESH,
        )

    def cedge_copy(side, d, src):
        to = (col + (1 if side == 0 else n_col - 1)) % n_col
        return pltpu.make_async_remote_copy(
            src_ref=coltail.at[side],
            dst_ref=coledge.at[side, src],
            send_sem=cedge_send.at[side, d],
            recv_sem=cedge_recv.at[side, src],
            device_id={"row": (row + d) % n_row, "col": to},
            device_id_type=MESH,
        )

    loop(1, n_row, lambda d: col_copy(d, row).start())
    loop(1, n_col, lambda d: row_copy(d, col).start())
    for side in range(2):
        loop(0, n_row, lambda d: cedge_copy(side, d, row).start())
        loop(0, n_col, lambda d: redge_copy(side, d, col).start())

    fetch.wait()
    inputs[4].wait()

    def widen(c, _):
        start = pl.multiple_of(c * edge, edge)
        target32[pl.ds(start, edge), :] = target_in[c].astype(F32)
        return 0

    lax.fori_loop(0, chan, widen, 0, unroll=4)
    for a in range(3):
        for b in range(3):
            weight_f[b * chan : (b + 1) * chan, a * chan : (a + 1) * chan] = conv_weight[
                a, b
            ].astype(F32)
    weight_t = weight_f[...].T.astype(BF16)
    out_t = pair_out[...].astype(F32).T
    pair_b = jnp.broadcast_to(pair_bias[...], (128, chan)).T
    conv_b = jnp.broadcast_to(conv_bias[...], (128, chan)).T
    zeros = jnp.zeros((2 * chan, 2 * edge), BF16)
    grad_in[0 : 2 * chan, :] = zeros
    grad_in[(pairs + 2) * chan : (pairs + 4) * chan, :] = zeros
    base[0 : 2 * chan, :] = zeros.astype(F32)
    base[(pairs + 2) * chan : (pairs + 4) * chan, :] = zeros.astype(F32)
    bias_acc[...] = jnp.zeros_like(bias_acc)
    total[...] = jnp.zeros_like(total)

    loop(1, n_row, lambda d: col_copy(d, (row + n_row - d) % n_row).wait_recv())
    loop(1, n_col, lambda d: row_copy(d, (col + n_col - d) % n_col).wait_recv())
    for side in range(2):
        loop(0, n_row, lambda d: cedge_copy(side, d, (row + n_row - d) % n_row).wait_recv())
        loop(0, n_col, lambda d: redge_copy(side, d, (col + n_col - d) % n_col).wait_recv())

    def summed(terms):
        return sum(x.astype(F32) for x in terms)

    row_feat[0:8, :] = rounded(summed(rowedge[0, c, 0:8, :] for c in range(n_col)))
    row_feat[8 : edge + 8, :] = rounded(summed(rowbuf[c, 0:rank, :] for c in range(n_col))).T
    row_feat[edge + 8 :, :] = rounded(summed(rowedge[1, c, 0:8, :] for c in range(n_col)))
    col_wide[0:8, :] = summed(coledge[0, r] for r in range(n_row))
    col_wide[8 : edge + 8, :] = summed(colbuf[r] for r in range(n_row)).T
    col_wide[edge + 8 :, :] = summed(coledge[1, r] for r in range(n_row))
    for b in range(3):
        wide_t[b * edge : (b + 1) * edge, :] = col_wide[
            6 + 2 * b : 6 + 2 * b + edge, :
        ].astype(BF16)

    lane = lax.broadcasted_iota(jnp.int32, (1, edge), 1)
    before, after = (col + n_col - 1) % n_col, (col + 1) % n_col
    has_before = (col > 0).astype(F32)
    has_after = (col < n_col - 1).astype(F32)

    def masks(get, valid):
        here, left, right = (
            jnp.broadcast_to(get(c), (1, edge)) * scale
            for c, scale in ((col, valid), (before, valid * has_before), (after, valid * has_after))
        )
        return (jnp.where(lane < 2, left, here), here, jnp.where(lane >= edge - 2, right, here))

    top = masks(lambda c: rowedge[0, c, 8:9, 0:1], (line > 0).astype(F32))
    middle = masks(lambda c: rowbuf[c, rank:, 0:1].astype(F32)[0:1], jnp.float32(1))
    bottom = masks(lambda c: rowedge[1, c, 8:9, 0:1], (line < n_line - 1).astype(F32))

    def features(pair, count, mask, inner):
        scaled = []
        for r in range(2 * count):
            feat = row_feat[pl.ds(2 * pair + 8 + r, 1), :]
            scaled.append((out_t * feat).astype(BF16))
        product = lax.dot_general(
            jnp.concatenate(scaled, axis=0), wide_t[...], NT, preferred_element_type=F32
        )
        for r in range(2 * count):
            p = pair + r // 2
            lanes = slice((r % 2) * edge, (r % 2 + 1) * edge)
            for b in range(3):
                value = product[r * chan : (r + 1) * chan, b * edge : (b + 1) * edge] + pair_b
                start = pl.multiple_of((p + 1) * 3 * chan + b * chan, chan)
                hid[pl.ds(start, chan), lanes] = (jnp.maximum(value, 0.0) * mask[b]).astype(BF16)
                if inner and b == 1:
                    aim = target32[pl.ds(2 * pair + r, chan, stride=edge), :]
                    start = pl.multiple_of((p + 2) * chan, chan)
                    base[pl.ds(start, chan), lanes] = (value + conv_b) - aim

    features(-1, 1, top, False)
    features(pairs, 1, bottom, False)
    group = 4

    def conv_of(p):
        start = pl.multiple_of((p + 1) * 3 * chan, 3 * chan)
        return jnp.dot(weight_t, hid[pl.ds(start, 3 * chan), :], preferred_element_type=F32)

    def slot(p):
        return pl.ds(pl.multiple_of((p + 2) * chan, chan), chan)

    def spread(p, done):
        y = conv_of(p)
        base[slot(p + 1), :] += y[0:chan]
        base[slot(p), :] += y[chan : 2 * chan]
        if done:
            differ = (base[slot(p - 1), :] + y[2 * chan :]) * keep
            grad_in[slot(p - 1), :] = differ.astype(BF16)
            bias_acc[...] += differ
            loss = 0.5 * jnp.sum(differ * differ, axis=0, keepdims=True)
            loss_out[pl.ds(2 * (p - 1), 1), :] = loss[:, 0:edge]
            loss_out[pl.ds(2 * (p - 1) + 1, 1), :] = loss[:, edge : 2 * edge]

    def grads(first, count):
        value = total[...]
        for r in range(count):
            p = first + r
            start = pl.multiple_of((p + 1) * 3 * chan, 3 * chan)
            near = pl.multiple_of((p + 1) * chan, chan)
            value = value + lax.dot_general(
                hid[pl.ds(start, 3 * chan), :],
                grad_in[pl.ds(near, 3 * chan), :],
                NT,
                preferred_element_type=F32,
            )
        total[...] = value

    for g in range(3):
        features(g * group, group, middle, True)
    spread(-1, False)
    spread(0, False)
    for r in range(group):
        spread(1 + r, True)
    lag = 2 * group - 1

    def step(g, _):
        grads(g * group - 3 * group - 1, group)
        for r in range(group):
            spread(g * group - lag + r, True)
        features(g * group, group, middle, True)
        return 0

    lax.fori_loop(3, pairs // group, step, 0)

    def conv_step(g, _):
        for r in range(group):
            spread(pairs - lag + g * group + r, True)
        return 0

    lax.fori_loop(0, 2, conv_step, 0)

    def grad_step(g, _):
        grads(pairs - 3 * group - 1 + g * 7, 7)
        return 0

    lax.fori_loop(0, 2, grad_step, 0)

    norm = 1.0 / (edge * edge)
    half = 3 * chan // 2
    rows = 3 * chan + half
    sums = total[...] * norm
    flat = jnp.concatenate(
        [
            sums[:, 0 : 2 * chan],
            jnp.concatenate([sums[0:half, 2 * chan :], sums[half:, 2 * chan :]], axis=1),
        ],
        axis=0,
    )
    bias_sum = lax.dot_general(
        jnp.ones((8, 2 * edge), F32),
        bias_acc[...] * norm,
        NT,
        precision=lax.Precision.HIGHEST,
        preferred_element_type=F32,
    )
    part[0:rows, :] = flat
    part[rows : rows + 8, :] = jnp.concatenate([bias_sum, bias_sum], axis=1)
    rest = n_all * chunk - rows - 8
    if rest > 0:
        part[rows + 8 :, :] = jnp.zeros((rest, 128), F32)

    def piece(index):
        return pl.ds(pl.multiple_of(index * chunk, 8), chunk)

    def rs_copy(d, to, src):
        return pltpu.make_async_remote_copy(
            src_ref=part.at[piece(to)],
            dst_ref=reduced.at[src],
            send_sem=rs_send.at[d],
            recv_sem=rs_recv.at[src],
            device_id=device(to),
            device_id_type=MESH,
        )

    def ag_copy(d, to, src):
        return pltpu.make_async_remote_copy(
            src_ref=full.at[src],
            dst_ref=full.at[src],
            send_sem=ag_send.at[d],
            recv_sem=ag_recv.at[src],
            device_id=device(to),
            device_id_type=MESH,
        )

    loop(1, n_all, lambda d: rs_copy(d, (me + d) % n_all, me).start())
    reduced[me] = part[piece(me), :]
    loop(1, n_all, lambda d: rs_copy(d, (me + d) % n_all, (me + n_all - d) % n_all).wait_recv())
    if n_all <= 16:
        own = sum(reduced[r] for r in range(n_all))
    else:
        own = lax.fori_loop(
            0, n_all, lambda r, x: x + reduced[r], jnp.zeros((chunk, 128), F32)
        )
    full[me] = own
    loop(1, n_all, lambda d: ag_copy(d, (me + d) % n_all, me).start())
    loop(1, n_all, lambda d: ag_copy(d, (me + d) % n_all, (me + n_all - d) % n_all).wait_recv())

    loop(1, n_row, lambda d: col_copy(d, row).wait_send())
    loop(1, n_col, lambda d: row_copy(d, col).wait_send())
    for side in range(2):
        loop(0, n_row, lambda d: cedge_copy(side, d, row).wait_send())
        loop(0, n_col, lambda d: redge_copy(side, d, col).wait_send())
    loop(1, n_all, lambda d: rs_copy(d, (me + d) % n_all, me).wait_send())
    loop(1, n_all, lambda d: ag_copy(d, (me + d) % n_all, me).wait_send())


def finish(loss_in, gathered, loss_out, conv_grad_out, bias_out, full):
    n_all, chunk = gathered.shape[0:2]

    def place(r):
        full[pl.ds(r * chunk, chunk), :] = gathered[r]

    loop(0, n_all, place)
    chan = bias_out.shape[1]
    half = 3 * chan // 2
    rows = 3 * chan + half
    loss_out[...] = loss_in[...]
    for b in range(3):
        low = b * chan
        conv_grad_out[2, b] = full[low : low + chan, 0:chan]
        conv_grad_out[1, b] = full[low : low + chan, chan : 2 * chan]
    low = 3 * chan
    conv_grad_out[0, 0] = full[low : low + chan, 0:chan]
    conv_grad_out[0, 1, 0 : half - chan] = full[low + chan : low + half, 0:chan]
    conv_grad_out[0, 1, half - chan :] = full[low : low + 2 * chan - half, chan : 2 * chan]
    conv_grad_out[0, 2] = full[low + 2 * chan - half : low + half, chan : 2 * chan]
    bias_out[...] = full[rows : rows + 1, 0:chan]


def solution(mesh):
    n_row, n_col, n_rep = (mesh.shape[axis] for axis in ("row", "col", "rep"))
    n_all = n_row * n_col * n_rep

    def per_device(
        emb_row,
        emb_col,
        proj_row,
        proj_col,
        pair_out,
        pair_bias,
        conv_weight,
        conv_bias,
        target,
        kept_tiles,
    ):
        chan, edge = target.shape[0], target.shape[1]
        rank = pair_out.shape[0]
        pairs = edge // 2
        used = 3 * chan + 3 * chan // 2 + 8
        chunk = 8 * pl.cdiv(used, 8 * n_all)

        dma = pltpu.SemaphoreType.DMA
        vmem = pl.BlockSpec(memory_space=pltpu.VMEM)
        hbm = pl.BlockSpec(memory_space=pl.ANY)
        loss, sums = pl.pallas_call(
            functools.partial(kernel, (n_row, n_col, n_rep, edge, chan, chunk)),
            out_shape=(
                jax.ShapeDtypeStruct((edge, edge), F32),
                jax.ShapeDtypeStruct((n_all, chunk, 128), F32),
            ),
            in_specs=[hbm] * 4
            + [vmem] * 2
            + [hbm, vmem, hbm, pl.BlockSpec(memory_space=pltpu.SMEM)],
            out_specs=(vmem,) * 2,
            scratch_shapes=[
                pltpu.VMEM(emb_row.shape, BF16),
                pltpu.VMEM(emb_col.shape[::-1], BF16),
                pltpu.VMEM(proj_row.shape[::-1], BF16),
                pltpu.VMEM(proj_col.shape[::-1], BF16),
                pltpu.VMEM(conv_weight.shape, BF16),
                dma((5,)),
                pltpu.VMEM((2, 16, rank), F32),
                pltpu.VMEM((2, 8, rank), F32),
                pltpu.VMEM((n_col, rank + 16, edge), BF16),
                pltpu.VMEM((2, n_col, 16, rank), F32),
                pltpu.VMEM((n_row, rank, edge), BF16),
                pltpu.VMEM((2, n_row, 8, rank), F32),
                pltpu.VMEM((edge + 16, rank), F32),
                pltpu.VMEM((edge + 16, rank), F32),
                pltpu.VMEM((3 * edge, rank), BF16),
                pltpu.VMEM((chan, edge, edge), BF16),
                pltpu.VMEM((chan * edge, edge), F32),
                pltpu.VMEM(((pairs + 2) * 3 * chan, 2 * edge), BF16),
                pltpu.VMEM(((pairs + 4) * chan, 2 * edge), F32),
                pltpu.VMEM(((pairs + 4) * chan, 2 * edge), BF16),
                pltpu.VMEM((3 * chan, 3 * chan), F32),
                pltpu.VMEM((3 * chan, 3 * chan), F32),
                pltpu.VMEM((chan, 2 * edge), F32),
                pltpu.VMEM((n_all * chunk, 128), F32),
                pltpu.VMEM((n_all, chunk, 128), F32),
                pltpu.SemaphoreType.DMA,
                dma((n_col,)),
                dma((n_col,)),
                dma((2, n_col)),
                dma((2, n_col)),
                dma((n_row,)),
                dma((n_row,)),
                dma((2, n_row)),
                dma((2, n_row)),
                dma((n_all,)),
                dma((n_all,)),
                dma((n_all,)),
                dma((n_all,)),
            ],
            compiler_params=pltpu.CompilerParams(collective_id=0, has_side_effects=True),
            name="pair_step",
        )(
            emb_row,
            emb_col.T,
            proj_row.T,
            proj_col.T,
            pair_out,
            pair_bias.reshape(1, chan),
            conv_weight,
            conv_bias.reshape(1, chan),
            target,
            kept_tiles,
        )
        loss, grads, bias = pl.pallas_call(
            finish,
            out_shape=(
                jax.ShapeDtypeStruct((edge, edge), F32),
                jax.ShapeDtypeStruct((3, 3, chan, chan), F32),
                jax.ShapeDtypeStruct((1, chan), F32),
            ),
            in_specs=[vmem] * 2,
            out_specs=(vmem,) * 3,
            scratch_shapes=[pltpu.VMEM((n_all * chunk, 128), F32)],
            name="finish",
        )(loss, sums)
        return loss, grads, bias.reshape(chan)

    in_specs = (
        P(("grp", "row", "rep"), "col"),
        P(("grp", "col"), "row"),
        P(),
        P(),
        P(),
        P(),
        P(),
        P(),
        P(None, ("grp", "row", "rep"), "col"),
        P(("grp", "row", "rep"), "col"),
    )
    out_specs = (P(("grp", "row", "rep"), "col"), P("grp", None, None, None), P("grp"))
    return jax.shard_map(
        per_device, mesh=mesh, in_specs=in_specs, out_specs=out_specs, check_vma=False
    )
```

```python
import functools

import jax
import jax.numpy as jnp
from jax import lax
from jax.experimental import pallas as pl
from jax.experimental.pallas import tpu as pltpu
from jax.sharding import PartitionSpec as P

MESH = pl.DeviceIdType.MESH
F32 = jnp.float32
BF16 = jnp.bfloat16
NT = (((1,), (1,)), ((), ()))


def loop(low, high, body):
    if high - low <= 16:
        for d in range(low, high):
            body(d)
    else:
        lax.fori_loop(low, high, lambda d, _: (body(d), 0)[1], 0)


def columns(ref, width, index, count):
    everything = ref.shape[1]
    if width % 128 == 0:
        return ref[:, pl.ds(pl.multiple_of(index * width, 128), width)]
    offset = max(i * width % 128 for i in range(count))
    window = min(-(-(offset + width) // 128) * 128, everything)
    tile = index * width // 128
    if any(i * width // 128 * 128 + window > everything for i in range(count)):
        tile = jnp.minimum(tile, (everything - window) // 128)
    value = ref[:, pl.ds(pl.multiple_of(tile * 128, 128), window)].astype(F32)
    shift = window - (index * width - tile * 128)
    return pltpu.roll(value, shift % window, 1)[:, 0:width].astype(BF16)


def kernel(
    sizes,
    emb_row_hbm,
    emb_col_hbm,
    proj_row_hbm,
    proj_col_hbm,
    pair_out,
    pair_bias,
    conv_weight_hbm,
    conv_bias,
    target,
    kept,
    loss_out,
    full,
    emb_row,
    emb_col,
    proj_row,
    proj_col,
    conv_weight,
    in_sem,
    rowtail,
    coltail,
    rowbuf,
    rowedge,
    colbuf,
    coledge,
    row_feat,
    col_wide,
    wide_t,
    target_in,
    target32,
    hid,
    base,
    grad_in,
    weight_f,
    total,
    bias_acc,
    part,
    reduced,
    target_sem,
    row_send,
    row_recv,
    redge_send,
    redge_recv,
    col_send,
    col_recv,
    cedge_send,
    cedge_recv,
    rs_send,
    rs_recv,
    ag_send,
    ag_recv,
):
    n_row, n_col, n_rep, edge, chan, chunk = sizes
    n_all = n_row * n_col * n_rep
    pairs = edge // 2
    row, col, rep = lax.axis_index("row"), lax.axis_index("col"), lax.axis_index("rep")
    line = row * n_rep + rep
    n_line = n_row * n_rep
    me = line * n_col + col

    def device(index):
        across = index % n_col
        along = index // n_col
        return {"row": along // n_rep, "rep": along % n_rep, "col": across}

    barrier = pltpu.get_barrier_semaphore()
    loop(
        1,
        n_all,
        lambda d: pl.semaphore_signal(
            barrier, inc=1, device_id=device((me + d) % n_all), device_id_type=MESH
        ),
    )

    inputs = [
        pltpu.make_async_copy(src, dst, in_sem.at[i])
        for i, (src, dst) in enumerate(
            (
                (emb_row_hbm, emb_row),
                (proj_row_hbm, proj_row),
                (emb_col_hbm, emb_col),
                (proj_col_hbm, proj_col),
                (conv_weight_hbm, conv_weight),
            )
        )
    ]
    for copy in inputs:
        copy.start()
    fetch = pltpu.make_async_copy(target, target_in, target_sem)
    fetch.start()

    def rounded(x):
        return x.astype(BF16).astype(F32)

    keep = kept[0, 0].astype(F32)
    for copy in inputs[2:4]:
        copy.wait()
    part_col = jnp.dot(
        columns(proj_col, emb_col.shape[0], row, n_row),
        emb_col[...],
        preferred_element_type=F32,
    )
    for copy in inputs[0:2]:
        copy.wait()
    part_row = lax.dot_general(
        columns(proj_row, emb_row.shape[1], col, n_col),
        emb_row[...],
        NT,
        preferred_element_type=F32,
    )
    rank = part_row.shape[0]
    colbuf[row] = part_col
    rowbuf[col, 0:rank, :] = part_row
    rowbuf[col, rank:, :] = jnp.full((8, edge), keep, F32)
    turned = part_col.T
    coltail[0] = turned[edge - 8 :]
    coltail[1] = turned[0:8]
    turned = part_row.T
    rowtail[0, 0:8] = turned[edge - 8 :]
    rowtail[1, 0:8] = turned[0:8]
    for side in range(2):
        rowtail[side, 8:16] = jnp.full((8, rank), keep, F32)

    pl.semaphore_wait(barrier, n_all - 1)

    def row_copy(d, src):
        return pltpu.make_async_remote_copy(
            src_ref=rowbuf.at[src],
            dst_ref=rowbuf.at[src],
            send_sem=row_send.at[d],
            recv_sem=row_recv.at[src],
            device_id={"col": (col + d) % n_col},
            device_id_type=MESH,
        )

    def redge_copy(side, d, src):
        to = (line + (1 if side == 0 else n_line - 1)) % n_line
        return pltpu.make_async_remote_copy(
            src_ref=rowtail.at[side],
            dst_ref=rowedge.at[side, src],
            send_sem=redge_send.at[side, d],
            recv_sem=redge_recv.at[side, src],
            device_id={"row": to // n_rep, "rep": to % n_rep, "col": (col + d) % n_col},
            device_id_type=MESH,
        )

    def col_copy(d, src):
        return pltpu.make_async_remote_copy(
            src_ref=colbuf.at[src],
            dst_ref=colbuf.at[src],
            send_sem=col_send.at[d],
            recv_sem=col_recv.at[src],
            device_id={"row": (row + d) % n_row},
            device_id_type=MESH,
        )

    def cedge_copy(side, d, src):
        to = (col + (1 if side == 0 else n_col - 1)) % n_col
        return pltpu.make_async_remote_copy(
            src_ref=coltail.at[side],
            dst_ref=coledge.at[side, src],
            send_sem=cedge_send.at[side, d],
            recv_sem=cedge_recv.at[side, src],
            device_id={"row": (row + d) % n_row, "col": to},
            device_id_type=MESH,
        )

    loop(1, n_row, lambda d: col_copy(d, row).start())
    loop(1, n_col, lambda d: row_copy(d, col).start())
    for side in range(2):
        loop(0, n_row, lambda d: cedge_copy(side, d, row).start())
        loop(0, n_col, lambda d: redge_copy(side, d, col).start())

    fetch.wait()
    inputs[4].wait()

    def widen(c, _):
        start = pl.multiple_of(c * edge, edge)
        target32[pl.ds(start, edge), :] = target_in[c].astype(F32)
        return 0

    lax.fori_loop(0, chan, widen, 0, unroll=4)
    for a in range(3):
        for b in range(3):
            weight_f[b * chan : (b + 1) * chan, a * chan : (a + 1) * chan] = conv_weight[
                a, b
            ].astype(F32)
    weight_t = weight_f[...].T.astype(BF16)
    out_t = pair_out[...].astype(F32).T
    pair_b = jnp.broadcast_to(pair_bias[...], (128, chan)).T
    conv_b = jnp.broadcast_to(conv_bias[...], (128, chan)).T
    zeros = jnp.zeros((2 * chan, 2 * edge), BF16)
    grad_in[0 : 2 * chan, :] = zeros
    grad_in[(pairs + 2) * chan : (pairs + 4) * chan, :] = zeros
    base[0 : 2 * chan, :] = zeros.astype(F32)
    base[(pairs + 2) * chan : (pairs + 4) * chan, :] = zeros.astype(F32)
    bias_acc[...] = jnp.zeros_like(bias_acc)
    total[...] = jnp.zeros_like(total)

    loop(1, n_row, lambda d: col_copy(d, (row + n_row - d) % n_row).wait_recv())
    loop(1, n_col, lambda d: row_copy(d, (col + n_col - d) % n_col).wait_recv())
    for side in range(2):
        loop(0, n_row, lambda d: cedge_copy(side, d, (row + n_row - d) % n_row).wait_recv())
        loop(0, n_col, lambda d: redge_copy(side, d, (col + n_col - d) % n_col).wait_recv())

    def summed(terms):
        return sum(terms)

    row_feat[0:8, :] = rounded(summed(rowedge[0, c, 0:8, :] for c in range(n_col)))
    row_feat[8 : edge + 8, :] = rounded(summed(rowbuf[c, 0:rank, :] for c in range(n_col))).T
    row_feat[edge + 8 :, :] = rounded(summed(rowedge[1, c, 0:8, :] for c in range(n_col)))
    col_wide[0:8, :] = summed(coledge[0, r] for r in range(n_row))
    col_wide[8 : edge + 8, :] = summed(colbuf[r] for r in range(n_row)).T
    col_wide[edge + 8 :, :] = summed(coledge[1, r] for r in range(n_row))
    for b in range(3):
        wide_t[b * edge : (b + 1) * edge, :] = col_wide[
            6 + 2 * b : 6 + 2 * b + edge, :
        ].astype(BF16)

    lane = lax.broadcasted_iota(jnp.int32, (1, edge), 1)
    before, after = (col + n_col - 1) % n_col, (col + 1) % n_col
    has_before = (col > 0).astype(F32)
    has_after = (col < n_col - 1).astype(F32)

    def masks(get, valid):
        here, left, right = (
            jnp.broadcast_to(get(c), (1, edge)) * scale
            for c, scale in ((col, valid), (before, valid * has_before), (after, valid * has_after))
        )
        return (jnp.where(lane < 2, left, here), here, jnp.where(lane >= edge - 2, right, here))

    top = masks(lambda c: rowedge[0, c, 8:9, 0:1], (line > 0).astype(F32))
    middle = masks(lambda c: rowbuf[c, rank : rank + 1, 0:1], jnp.float32(1))
    bottom = masks(lambda c: rowedge[1, c, 8:9, 0:1], (line < n_line - 1).astype(F32))

    def features(pair, count, mask, inner):
        scaled = []
        for r in range(2 * count):
            feat = row_feat[pl.ds(2 * pair + 8 + r, 1), :]
            scaled.append((out_t * feat).astype(BF16))
        product = lax.dot_general(
            jnp.concatenate(scaled, axis=0), wide_t[...], NT, preferred_element_type=F32
        )
        for r in range(2 * count):
            p = pair + r // 2
            lanes = slice((r % 2) * edge, (r % 2 + 1) * edge)
            for b in range(3):
                value = product[r * chan : (r + 1) * chan, b * edge : (b + 1) * edge] + pair_b
                start = pl.multiple_of((p + 1) * 3 * chan + b * chan, chan)
                hid[pl.ds(start, chan), lanes] = (jnp.maximum(value, 0.0) * mask[b]).astype(BF16)
                if inner and b == 1:
                    aim = target32[pl.ds(2 * pair + r, chan, stride=edge), :]
                    start = pl.multiple_of((p + 2) * chan, chan)
                    base[pl.ds(start, chan), lanes] = (value + conv_b) - aim

    features(-1, 1, top, False)
    features(pairs, 1, bottom, False)
    group = 4

    def conv_of(p):
        start = pl.multiple_of((p + 1) * 3 * chan, 3 * chan)
        return jnp.dot(weight_t, hid[pl.ds(start, 3 * chan), :], preferred_element_type=F32)

    def slot(p):
        return pl.ds(pl.multiple_of((p + 2) * chan, chan), chan)

    def spread(p, done):
        y = conv_of(p)
        base[slot(p + 1), :] += y[0:chan]
        base[slot(p), :] += y[chan : 2 * chan]
        if done:
            differ = (base[slot(p - 1), :] + y[2 * chan :]) * keep
            grad_in[slot(p - 1), :] = differ.astype(BF16)
            bias_acc[...] += differ
            loss = 0.5 * jnp.sum(differ * differ, axis=0, keepdims=True)
            loss_out[pl.ds(2 * (p - 1), 1), :] = loss[:, 0:edge]
            loss_out[pl.ds(2 * (p - 1) + 1, 1), :] = loss[:, edge : 2 * edge]

    def grads(first, count):
        value = total[...]
        for r in range(count):
            p = first + r
            start = pl.multiple_of((p + 1) * 3 * chan, 3 * chan)
            near = pl.multiple_of((p + 1) * chan, chan)
            value = value + lax.dot_general(
                hid[pl.ds(start, 3 * chan), :],
                grad_in[pl.ds(near, 3 * chan), :],
                NT,
                preferred_element_type=F32,
            )
        total[...] = value

    for g in range(3):
        features(g * group, group, middle, True)
    spread(-1, False)
    spread(0, False)
    for r in range(group):
        spread(1 + r, True)
    lag = 2 * group - 1

    def step(g, _):
        grads(g * group - 3 * group - 1, group)
        for r in range(group):
            spread(g * group - lag + r, True)
        features(g * group, group, middle, True)
        return 0

    lax.fori_loop(3, pairs // group, step, 0)

    def conv_step(g, _):
        for r in range(group):
            spread(pairs - lag + g * group + r, True)
        return 0

    lax.fori_loop(0, 2, conv_step, 0)

    def grad_step(g, _):
        grads(pairs - 3 * group - 1 + g * 7, 7)
        return 0

    lax.fori_loop(0, 2, grad_step, 0)

    norm = 1.0 / (edge * edge)
    half = 3 * chan // 2
    rows = 3 * chan + half
    sums = total[...] * norm
    flat = jnp.concatenate(
        [
            sums[:, 0 : 2 * chan],
            jnp.concatenate([sums[0:half, 2 * chan :], sums[half:, 2 * chan :]], axis=1),
        ],
        axis=0,
    )
    bias_sum = lax.dot_general(
        jnp.ones((8, 2 * edge), F32),
        bias_acc[...] * norm,
        NT,
        precision=lax.Precision.HIGHEST,
        preferred_element_type=F32,
    )
    part[0:rows, :] = flat
    part[rows : rows + 8, :] = jnp.concatenate([bias_sum, bias_sum], axis=1)
    rest = n_all * chunk - rows - 8
    if rest > 0:
        part[rows + 8 :, :] = jnp.zeros((rest, 128), F32)

    def piece(index):
        return pl.ds(pl.multiple_of(index * chunk, 8), chunk)

    def rs_copy(d, to, src):
        return pltpu.make_async_remote_copy(
            src_ref=part.at[piece(to)],
            dst_ref=reduced.at[src],
            send_sem=rs_send.at[d],
            recv_sem=rs_recv.at[src],
            device_id=device(to),
            device_id_type=MESH,
        )

    def ag_copy(d, to, src):
        return pltpu.make_async_remote_copy(
            src_ref=full.at[src],
            dst_ref=full.at[src],
            send_sem=ag_send.at[d],
            recv_sem=ag_recv.at[src],
            device_id=device(to),
            device_id_type=MESH,
        )

    loop(1, n_all, lambda d: rs_copy(d, (me + d) % n_all, me).start())
    reduced[me] = part[piece(me), :]
    loop(1, n_all, lambda d: rs_copy(d, (me + d) % n_all, (me + n_all - d) % n_all).wait_recv())
    if n_all <= 16:
        own = sum(reduced[r] for r in range(n_all))
    else:
        own = lax.fori_loop(
            0, n_all, lambda r, x: x + reduced[r], jnp.zeros((chunk, 128), F32)
        )
    full[me] = own
    loop(1, n_all, lambda d: ag_copy(d, (me + d) % n_all, me).start())
    loop(1, n_all, lambda d: ag_copy(d, (me + d) % n_all, (me + n_all - d) % n_all).wait_recv())

    loop(1, n_row, lambda d: col_copy(d, row).wait_send())
    loop(1, n_col, lambda d: row_copy(d, col).wait_send())
    for side in range(2):
        loop(0, n_row, lambda d: cedge_copy(side, d, row).wait_send())
        loop(0, n_col, lambda d: redge_copy(side, d, col).wait_send())
    loop(1, n_all, lambda d: rs_copy(d, (me + d) % n_all, me).wait_send())
    loop(1, n_all, lambda d: ag_copy(d, (me + d) % n_all, me).wait_send())


def finish(loss_in, gathered, loss_out, conv_grad_out, bias_out, full):
    n_all, chunk = gathered.shape[0:2]

    def place(r):
        full[pl.ds(r * chunk, chunk), :] = gathered[r]

    loop(0, n_all, place)
    chan = bias_out.shape[1]
    half = 3 * chan // 2
    rows = 3 * chan + half
    loss_out[...] = loss_in[...]
    for b in range(3):
        low = b * chan
        conv_grad_out[2, b] = full[low : low + chan, 0:chan]
        conv_grad_out[1, b] = full[low : low + chan, chan : 2 * chan]
    low = 3 * chan
    conv_grad_out[0, 0] = full[low : low + chan, 0:chan]
    conv_grad_out[0, 1, 0 : half - chan] = full[low + chan : low + half, 0:chan]
    conv_grad_out[0, 1, half - chan :] = full[low : low + 2 * chan - half, chan : 2 * chan]
    conv_grad_out[0, 2] = full[low + 2 * chan - half : low + half, chan : 2 * chan]
    bias_out[...] = full[rows : rows + 1, 0:chan]


def solution(mesh):
    n_row, n_col, n_rep = (mesh.shape[axis] for axis in ("row", "col", "rep"))
    n_all = n_row * n_col * n_rep

    def per_device(
        emb_row,
        emb_col,
        proj_row,
        proj_col,
        pair_out,
        pair_bias,
        conv_weight,
        conv_bias,
        target,
        kept_tiles,
    ):
        chan, edge = target.shape[0], target.shape[1]
        rank = pair_out.shape[0]
        pairs = edge // 2
        used = 3 * chan + 3 * chan // 2 + 8
        chunk = 8 * pl.cdiv(used, 8 * n_all)

        dma = pltpu.SemaphoreType.DMA
        vmem = pl.BlockSpec(memory_space=pltpu.VMEM)
        hbm = pl.BlockSpec(memory_space=pl.ANY)
        loss, sums = pl.pallas_call(
            functools.partial(kernel, (n_row, n_col, n_rep, edge, chan, chunk)),
            out_shape=(
                jax.ShapeDtypeStruct((edge, edge), F32),
                jax.ShapeDtypeStruct((n_all, chunk, 128), F32),
            ),
            in_specs=[hbm] * 4
            + [vmem] * 2
            + [hbm, vmem, hbm, pl.BlockSpec(memory_space=pltpu.SMEM)],
            out_specs=(vmem,) * 2,
            scratch_shapes=[
                pltpu.VMEM(emb_row.shape, BF16),
                pltpu.VMEM(emb_col.shape[::-1], BF16),
                pltpu.VMEM(proj_row.shape[::-1], BF16),
                pltpu.VMEM(proj_col.shape[::-1], BF16),
                pltpu.VMEM(conv_weight.shape, BF16),
                dma((5,)),
                pltpu.VMEM((2, 16, rank), F32),
                pltpu.VMEM((2, 8, rank), F32),
                pltpu.VMEM((n_col, rank + 8, edge), F32),
                pltpu.VMEM((2, n_col, 16, rank), F32),
                pltpu.VMEM((n_row, rank, edge), F32),
                pltpu.VMEM((2, n_row, 8, rank), F32),
                pltpu.VMEM((edge + 16, rank), F32),
                pltpu.VMEM((edge + 16, rank), F32),
                pltpu.VMEM((3 * edge, rank), BF16),
                pltpu.VMEM((chan, edge, edge), BF16),
                pltpu.VMEM((chan * edge, edge), F32),
                pltpu.VMEM(((pairs + 2) * 3 * chan, 2 * edge), BF16),
                pltpu.VMEM(((pairs + 4) * chan, 2 * edge), F32),
                pltpu.VMEM(((pairs + 4) * chan, 2 * edge), BF16),
                pltpu.VMEM((3 * chan, 3 * chan), F32),
                pltpu.VMEM((3 * chan, 3 * chan), F32),
                pltpu.VMEM((chan, 2 * edge), F32),
                pltpu.VMEM((n_all * chunk, 128), F32),
                pltpu.VMEM((n_all, chunk, 128), F32),
                pltpu.SemaphoreType.DMA,
                dma((n_col,)),
                dma((n_col,)),
                dma((2, n_col)),
                dma((2, n_col)),
                dma((n_row,)),
                dma((n_row,)),
                dma((2, n_row)),
                dma((2, n_row)),
                dma((n_all,)),
                dma((n_all,)),
                dma((n_all,)),
                dma((n_all,)),
            ],
            compiler_params=pltpu.CompilerParams(collective_id=0, has_side_effects=True),
            name="pair_step",
        )(
            emb_row,
            emb_col.T,
            proj_row.T,
            proj_col.T,
            pair_out,
            pair_bias.reshape(1, chan),
            conv_weight,
            conv_bias.reshape(1, chan),
            target,
            kept_tiles,
        )
        loss, grads, bias = pl.pallas_call(
            finish,
            out_shape=(
                jax.ShapeDtypeStruct((edge, edge), F32),
                jax.ShapeDtypeStruct((3, 3, chan, chan), F32),
                jax.ShapeDtypeStruct((1, chan), F32),
            ),
            in_specs=[vmem] * 2,
            out_specs=(vmem,) * 3,
            scratch_shapes=[pltpu.VMEM((n_all * chunk, 128), F32)],
            name="finish",
        )(loss, sums)
        return loss, grads, bias.reshape(chan)

    in_specs = (
        P(("grp", "row", "rep"), "col"),
        P(("grp", "col"), "row"),
        P(),
        P(),
        P(),
        P(),
        P(),
        P(),
        P(None, ("grp", "row", "rep"), "col"),
        P(("grp", "row", "rep"), "col"),
    )
    out_specs = (P(("grp", "row", "rep"), "col"), P("grp", None, None, None), P("grp"))
    return jax.shard_map(
        per_device, mesh=mesh, in_specs=in_specs, out_specs=out_specs, check_vma=False
    )
```
